32 devices in a mesh: group: 2 (over y), inner: 4 (over z), outer: 2 (over x), cuts: 2 (over core).
Axes of the slice: x: 2, y: 2, z: 4, core: 2. Of those that a mesh axis runs over, the one named last changes fastest.
Arguments:
- volume: bfloat16 [96, 128, 256], P(('group', 'inner', 'outer'), None, 'cuts'), parts along dimension 0, may hold values from -6 to 6
- projector: bfloat16 [256, 4, 128, 128], P(('inner', 'outer')), may hold values from 0.19921875 to 1
- slot_ray: int32 [256], P(('inner', 'outer')), may hold values from 0 to 63, as said below
- slot_pixel: int32 [256, 4], P(('inner', 'outer')), may hold values from 0 to 5, as said below
- sinogram: bfloat16 [128, 128, 256], P(('group', 'inner', 'outer'), None, 'cuts'), parts along dimension 0, may hold values from -240 to 240
- weight_index: int32 [128, 128], P(('group', 'inner', 'outer')), parts along dimension 0, may hold values from 0 to 15
- weight_table: bfloat16 [16], replicated, may hold values from 0.099609375 to 1
Outputs:
- updated: float32 [96, 128, 256], P(('group', 'inner', 'outer'), None, 'cuts'), parts along dimension 0
The draws below stay inside these ranges and needn't reach their ends.
There are 2 independent parts, one for each index of `group`. The reference program is written for one: setup_inputs(seed, part) draws one part's arguments, and reference() takes and returns one part's arrays. A program takes and returns all parts, laid end to end along the dimension named above; an argument that names none is the same for every part. Nothing has to cross between parts.
Inputs may be any that keep to these rules, and one draw needn't show every extreme that they name: `slot_ray`: each patch lists 32 ray tiles, possibly some more than once. At most 16 of one patch's slots name ray tiles of one band k * 16 to (k + 1) * 16 - 1, and in every draw some band receives exactly 16 slots from every patch. `slot_pixel`: the 4 entries of a slot are different pixel tiles of its own patch; every pixel tile of a patch is named by some slot of that patch.
All inputs are finite; a program needn't handle non-finite values.
Results may differ from the reference program's by a relative error of at most 0.0003.
Values may be sent and summed in bfloat16 or wider, within the bound.
A program may use at most 64 MiB of HBM per device.

```python
import math
import jax
import jax.numpy as jnp
from jax import lax

TILE = 128
PATCH_TILES = 6
SLOTS_DEV = 32
TILES_SLOT = 4
CLASSES = 16
PIX_TILES = 48
SLOTS = 256
RAY_TILES = 64
BAND = 16
CAPACITY = 16
SLICES = 256
N_INNER = 4
N_OUTER = 2


def draw_slot_ray(key, part):
    base_key = jax.random.fold_in(key, 101)
    key_hot, key_score, key_offset, key_order = jax.random.split(base_key, 4)
    patches = N_INNER * N_OUTER
    cell_count = N_INNER * CAPACITY
    hot_inner = jax.random.randint(key_hot, (), 0, N_INNER)
    cell_index = jnp.arange(cell_count, dtype=jnp.int32)
    dest_inner = cell_index // CAPACITY
    scores = jax.random.randint(key_score, (patches, cell_count), 0, 2 ** 16) * cell_count + cell_index[None, :]
    scores = scores + jnp.where(dest_inner == hot_inner, 2 ** 29, 0).astype(jnp.int32)[None, :]
    chosen = lax.top_k(scores, SLOTS_DEV)[1]
    order_scores = jax.random.randint(key_order, (patches, SLOTS_DEV), 0, 2 ** 16) * SLOTS_DEV + jnp.arange(SLOTS_DEV, dtype=jnp.int32)[None, :]
    shuffle = lax.top_k(order_scores, SLOTS_DEV)[1]
    chosen = jnp.take_along_axis(chosen, shuffle, axis=1)
    offsets = jax.random.randint(key_offset, (patches, SLOTS_DEV), 0, BAND)
    ray_rows = chosen // CAPACITY * BAND + offsets
    return ray_rows.reshape(-1).astype(jnp.int32)


def draw_slot_pixel(key, part):
    base_key = jax.random.fold_in(key, 202)
    slot_total = N_INNER * N_OUTER * SLOTS_DEV
    scores = jax.random.randint(base_key, (slot_total, PATCH_TILES), 0, 2 ** 16) * PATCH_TILES + jnp.arange(PATCH_TILES, dtype=jnp.int32)[None, :]
    shuffle = lax.top_k(scores, PATCH_TILES)[1]
    leading = shuffle[:, :1]
    wanted = (jnp.arange(slot_total, dtype=jnp.int32) % SLOTS_DEV % PATCH_TILES)[:, None]
    rolled = (shuffle - leading + wanted) % PATCH_TILES
    return rolled[:, :TILES_SLOT].astype(jnp.int32)


def set_ends(array, rng, low, top_value):
    longest = array.shape.index(max(array.shape))
    spots = []
    for shift in (0, 1):
        where = [jax.random.randint(jax.random.fold_in(rng, axis), (), 0, length) for axis, length in enumerate(array.shape)]
        where[longest] = (where[longest] + shift) % array.shape[longest]
        spots.append(tuple(where))
    return array.at[spots[0]].set(low).at[spots[1]].set(top_value)


def shard_levels(stream_key, extent, cuts, smallest, top_value):
    factor_of, own = 1.0, jax.random.fold_in(stream_key, 6)
    for dim, parts in cuts:
        heights = jnp.exp(jax.random.uniform(jax.random.fold_in(own, dim), (parts,), jnp.float32, smallest / len(cuts), top_value / len(cuts)))
        factor_of = factor_of * jnp.repeat(heights, extent[dim] // parts).reshape([-1 if axis == dim else 1 for axis in range(len(extent))])
    return factor_of


def centred(stream_key, extent, deviation, reach, cuts=(), kind=jnp.bfloat16):
    entries = deviation * jax.random.normal(stream_key, extent, jnp.float32)
    if cuts:
        entries = entries * shard_levels(stream_key, extent, cuts, -0.22, 0.18)
    return jnp.clip(entries, -reach, reach).astype(kind)


def setup_inputs(seed: int = 0, part: int = 0) -> dict:
    arg_keys = jax.random.split(jax.random.key(seed), 8)
    part_splits = jax.random.split(jax.random.fold_in(arg_keys[7], part), 8)
    volume = centred(part_splits[0], (PIX_TILES, TILE, SLICES), 1.0, 6.0, ((0, 8), (2, 2)))
    projector = jnp.clip(0.19921875 + 0.80078125 * jax.random.uniform(arg_keys[1], (SLOTS, TILES_SLOT, TILE, TILE), jnp.float32) ** shard_levels(arg_keys[1], (SLOTS, TILES_SLOT, TILE, TILE), ((0, 8),), -0.2, 0.2), 0.19921875, 1.0).astype(jnp.bfloat16)
    slot_ray = draw_slot_ray(jax.random.fold_in(arg_keys[7], 71), part)
    slot_pixel = draw_slot_pixel(jax.random.fold_in(arg_keys[7], 71), part)
    sinogram = centred(part_splits[4], (RAY_TILES, TILE, SLICES), 40.0, 240.0, ((0, 8), (2, 2)))
    weight_index = set_ends(jax.random.randint(part_splits[5], (RAY_TILES, TILE), 0, CLASSES), jax.random.fold_in(part_splits[5], 1), 0, CLASSES - 1).astype(jnp.int32)
    weight_table = jnp.clip(jnp.exp(jax.random.uniform(arg_keys[6], (CLASSES,), jnp.float32, math.log(0.099609375), math.log(1.0))), 0.099609375, 1.0).astype(jnp.bfloat16)
    return {"volume": volume, "projector": projector, "slot_ray": slot_ray, "slot_pixel": slot_pixel, "sinogram": sinogram, "weight_index": weight_index, "weight_table": weight_table}


def reference(volume, projector, slot_ray, slot_pixel, sinogram, weight_index, weight_table):
    patches = N_INNER * N_OUTER
    slot_count = projector.shape[0] // patches
    per_slot = projector.shape[1]
    tile_size = projector.shape[2]
    patch_tiles = volume.shape[0] // patches
    slice_count = volume.shape[2]
    ray_count = sinogram.shape[0]
    patch_base = (jnp.arange(projector.shape[0], dtype=jnp.int32) // slot_count) * patch_tiles
    pixel_index = (patch_base[:, None] + slot_pixel).astype(jnp.int32)
    grouped = (projector.reshape(patches, slot_count, per_slot, tile_size, tile_size),
               slot_ray.reshape(patches, slot_count).astype(jnp.int32),
               pixel_index.reshape(patches, slot_count, per_slot))

    def forward(running, pieces):
        tiles_here, rays_here, pixels_here = pieces
        gathered = volume[pixels_here].astype(jnp.float32)
        partial_value = jnp.einsum("sgrp,sgpc->src", tiles_here.astype(jnp.float32), gathered,
                             precision=lax.Precision.HIGHEST)
        return running.at[rays_here].add(partial_value), None

    projection = lax.scan(forward, jnp.zeros((ray_count, tile_size, slice_count), jnp.float32), grouped)[0]
    weights = weight_table[weight_index].astype(jnp.float32)
    residual = (weights[:, :, None] * (sinogram.astype(jnp.float32) - projection)).astype(jnp.bfloat16)

    def backward(running, pieces):
        totals, column_sum = running
        tiles_here, rays_here, pixels_here = pieces
        tiles_wide = tiles_here.astype(jnp.float32)
        spread = jnp.einsum("sgrp,src->sgpc", tiles_wide, residual[rays_here].astype(jnp.float32),
                            precision=lax.Precision.HIGHEST)
        flat_pixels = pixels_here.reshape(-1)
        totals = totals.at[flat_pixels].add(spread.reshape(-1, tile_size, slice_count))
        column_sum = column_sum.at[flat_pixels].add(jnp.sum(tiles_wide, axis=2).reshape(-1, tile_size))
        return (totals, column_sum), None

    start = (jnp.zeros((volume.shape[0], tile_size, slice_count), jnp.float32),
             jnp.zeros((volume.shape[0], tile_size), jnp.float32))
    carried = lax.scan(backward, start, grouped)[0]
    return volume.astype(jnp.float32) + carried[0] / carried[1][:, :, None]
```

```python
import functools

import jax
import jax.numpy as jnp
from jax import lax
from jax.experimental import pallas as pl
from jax.experimental.pallas import tpu as pltpu
from jax.sharding import PartitionSpec as P

MESH = pl.DeviceIdType.MESH
PIECE = 16


def general_path(volume, projector, slot_ray, slot_pixel, sinogram, weight_index, weight_table):
    inners = lax.axis_size("inner")
    outers = lax.axis_size("outer")
    slot_count = projector.shape[0]
    per_slot = projector.shape[1]
    tile_rows = projector.shape[2]
    tile_cols = projector.shape[3]
    patch_tiles = volume.shape[0]
    slice_count = volume.shape[2]
    owned_rows = sinogram.shape[0]
    band_rows = owned_rows * outers
    capacity = 2 * slot_count // inners
    cell_count = inners * capacity
    target = slot_ray // band_rows
    offset = slot_ray % band_rows
    same_target = target[:, None] == target[None, :]
    earlier = jnp.arange(slot_count)[:, None] > jnp.arange(slot_count)[None, :]
    slot_rank = jnp.sum(jnp.logical_and(same_target, earlier), axis=1)
    position = target * capacity + slot_rank
    partial_value = jnp.zeros((slot_count, tile_rows, slice_count), jnp.float32)
    for column in range(per_slot):
        pixels = volume[slot_pixel[:, column]]
        partial_value = partial_value + jnp.einsum(
            "srp,spc->src", projector[:, column], pixels, preferred_element_type=jnp.float32
        )
    outgoing = (
        jnp.zeros((cell_count, tile_rows, slice_count), jnp.float32).at[position].set(partial_value)
    )
    labels = jnp.full((cell_count,), -1.0, jnp.float32).at[position].set(offset.astype(jnp.float32))
    arrived, arrived_rows = (
        lax.all_to_all(
            outgoing.reshape(inners, capacity, tile_rows, slice_count),
            "inner",
            split_axis=0,
            concat_axis=0,
            tiled=True,
        ),
        lax.all_to_all(
            labels.reshape(inners, capacity), "inner", split_axis=0, concat_axis=0, tiled=True
        ),
    )
    selector = (
        jnp.arange(band_rows, dtype=jnp.float32)[:, None] == arrived_rows.reshape(1, cell_count)
    ).astype(jnp.float32)
    block_sums = jnp.dot(
        selector,
        arrived.reshape(cell_count, tile_rows * slice_count),
        precision=lax.Precision.HIGHEST,
    ).reshape(band_rows, tile_rows, slice_count)
    classes = weight_table.shape[0]
    lookup = weight_index[:, :, None] == jnp.arange(classes)[None, None, :]
    weights = jnp.sum(
        jnp.where(lookup, weight_table[None, None, :], jnp.zeros((), weight_table.dtype)), axis=2
    )
    own_sums = lax.psum_scatter(block_sums, "outer", scatter_dimension=0, tiled=True)
    own_residual = (
        weights.astype(jnp.float32)[:, :, None] * (sinogram.astype(jnp.float32) - own_sums)
    ).astype(jnp.bfloat16)
    residual = lax.all_gather(own_residual, "outer", axis=0, tiled=True)
    picked = jnp.dot(
        selector.T.astype(jnp.bfloat16),
        residual.reshape(band_rows, tile_rows * slice_count),
        preferred_element_type=jnp.float32,
    ).astype(jnp.bfloat16)
    returned = lax.all_to_all(
        picked.reshape(inners, capacity, tile_rows, slice_count),
        "inner",
        split_axis=0,
        concat_axis=0,
        tiled=True,
    )
    slot_residual = returned.reshape(cell_count, tile_rows, slice_count)[position]
    owners = jnp.arange(patch_tiles)
    backward = jnp.zeros((patch_tiles, tile_cols, slice_count), jnp.float32)
    column_sum = jnp.zeros((patch_tiles, tile_cols), jnp.float32)
    for column in range(per_slot):
        member = (owners[:, None] == slot_pixel[None, :, column]).astype(jnp.float32)
        spread = jnp.einsum(
            "srp,src->spc", projector[:, column], slot_residual, preferred_element_type=jnp.float32
        )
        backward = backward + jnp.einsum(
            "ts,spc->tpc", member, spread, precision=lax.Precision.HIGHEST
        )
        column_sum = column_sum + jnp.dot(
            member,
            jnp.sum(projector[:, column], axis=1, dtype=jnp.float32),
            precision=lax.Precision.HIGHEST,
        )
    return volume.astype(jnp.float32) + backward / column_sum[:, :, None]


def forward_kernel(first_ref, pixel_ref, volume_ref, projector_ref, packed_ref):
    step = pl.program_id(0)
    block, per_slot = projector_ref.shape[:2]

    @pl.when(step == 0)
    def _():
        packed_ref[...] = jnp.zeros_like(packed_ref)

    for j in range(block):
        s = step * block + j
        pixels = jnp.concatenate(
            [volume_ref[pixel_ref[s * per_slot + g]] for g in range(per_slot)], axis=0
        )
        tiles = jnp.concatenate([projector_ref[j, g] for g in range(per_slot)], axis=1)
        packed_ref[first_ref[s]] += jnp.dot(tiles, pixels, preferred_element_type=jnp.float32)


def backward_kernel(pixel_ref, volume_ref, projector_ref, residual_ref, out_ref, acc_ref):
    step = pl.program_id(0)
    block, per_slot, rows, cols = projector_ref.shape
    slices = residual_ref.shape[-1]

    @pl.when(step == 0)
    def _():
        acc_ref[...] = jnp.zeros_like(acc_ref)

    ones = jnp.ones((rows, slices), jnp.bfloat16)
    for j in range(block):
        s = step * block + j
        wide = jnp.concatenate([residual_ref[j], ones], axis=1)
        tiles = jnp.concatenate([projector_ref[j, g] for g in range(per_slot)], axis=1)
        spread = lax.dot_general(
            tiles, wide, (((0,), (0,)), ((), ())), preferred_element_type=jnp.float32
        )
        for g in range(per_slot):
            acc_ref[pixel_ref[s * per_slot + g]] += spread[g * cols : (g + 1) * cols]

    @pl.when(step == pl.num_programs(0) - 1)
    def _():
        out_ref[...] = (
            volume_ref[...].astype(jnp.float32) + acc_ref[:, :, :slices] / acc_ref[:, :, slices:]
        )


def exchange_kernel(n, pieces, own_idx, mate_idx, packed, sino, wts, out_ref, *scratch):
    take = iter(scratch)
    mate_part = [next(take) for _ in range(pieces)]
    from_left, from_right, going, total = (next(take) for _ in range(4))
    band_res = [next(take) for _ in range(pieces)]
    picked = [next(take) for _ in range(pieces)]
    landed = [next(take) for _ in range(pieces)]
    mate_sino, mate_wts = next(take), next(take)
    x_send, x_recv, aux_send, aux_recv, sum_send, left_recv, right_recv = (
        next(take) for _ in range(7)
    )
    out_right, out_left, res_recv, pick_send, pick_recv = (next(take) for _ in range(5))

    slots, rows, slices = out_ref.shape
    owned = sino.shape[0]
    band = 2 * owned
    half = rows // 2
    depth = half // pieces
    i = lax.axis_index("inner")
    o = lax.axis_index("outer")
    mate = {"outer": 1 - o}
    right = {"inner": i + 1}
    left = {"inner": i - 1}

    def send(src, dst, ssem, rsem, device):
        return pltpu.make_async_remote_copy(
            src_ref=src, dst_ref=dst, send_sem=ssem, recv_sem=rsem, device_id=device,
            device_id_type=MESH,
        )

    barrier = pltpu.get_barrier_semaphore()
    pl.semaphore_signal(barrier, inc=1, device_id=mate, device_id_type=MESH)

    @pl.when(i > 0)
    def _():
        pl.semaphore_signal(barrier, inc=1, device_id=left, device_id_type=MESH)

    @pl.when(i < n - 1)
    def _():
        pl.semaphore_signal(barrier, inc=1, device_id=right, device_id_type=MESH)

    pl.semaphore_wait(barrier, jnp.where(i > 0, 2, 1) + jnp.where(i < n - 1, 1, 0))

    def mine(c):
        return pl.ds(pl.multiple_of(o * half + c * depth, depth), depth)

    def theirs(c):
        return pl.ds(pl.multiple_of((1 - o) * half + c * depth, depth), depth)

    def swap(c):
        return send(
            packed.at[pl.ds(0, slots), theirs(c)],
            mate_part[c].at[pl.ds(0, slots)],
            x_send.at[c],
            x_recv.at[c],
            mate,
        )

    other_half = pl.ds(pl.multiple_of((1 - o) * half, half), half)
    aux = [
        send(sino.at[:, other_half], mate_sino, aux_send.at[0], aux_recv.at[0], mate),
        send(wts.at[other_half], mate_wts, aux_send.at[1], aux_recv.at[1], mate),
    ]
    for c in range(pieces):
        swap(c).start()
        if c == min(1, pieces - 1):
            for copy in aux:
                copy.start()
    for c in range(pieces):
        mate_part[c][slots] = jnp.zeros((depth, slices), jnp.float32)

    def local(c, r):
        return packed[own_idx[slots + r], mine(c), :] + mate_part[c][mate_idx[slots + r]]

    def loop(count, body):
        def step(t, carry):
            body(t)
            return carry

        lax.fori_loop(0, count, step, 0, unroll=4)

    def go_right(c, b):
        return send(
            going.at[c, b], from_left.at[c, b], sum_send.at[c, b], left_recv.at[c, b], right
        )

    def go_left(c, b):
        return send(
            going.at[c, b], from_right.at[c, b], sum_send.at[c, b], right_recv.at[c, b], left
        )

    def sums(c):
        swap(c).wait_recv()

        def one(b, to_right):
            def fill(t):
                going[c, b, t] = local(c, b * band + t)

            loop(band, fill)
            inner_side = i > 0 if to_right else i < n - 1
            arrived = from_left if to_right else from_right

            @pl.when(inner_side)
            def _():
                (go_right if to_right else go_left)(c, b).wait_recv()

                def add(t):
                    going[c, b, t] += arrived[c, b, t]

                loop(band, add)

            (go_right if to_right else go_left)(c, b).start()

        for far in range(n - 1):
            b = n - 1 - far
            pl.when(b > i)(functools.partial(one, b, True))
            pl.when(far < i)(functools.partial(one, far, False))

    def share_right(c, b):
        part = band_res[c].at[pl.ds(pl.multiple_of(b * band, band), band)]
        return send(part, part, out_right.at[c, b], res_recv.at[c, b], right)

    def share_left(c, b):
        part = band_res[c].at[pl.ds(pl.multiple_of(b * band, band), band)]
        return send(part, part, out_left.at[c, b], res_recv.at[c, b], left)

    def finish(c):
        def start_total(t):
            total[t] = local(c, i * band + t)

        loop(band, start_total)

        @pl.when(i > 0)
        def _():
            go_right(c, i).wait_recv()

            def add(t):
                total[t] += from_left[c, i, t]

            loop(band, add)

        @pl.when(i < n - 1)
        def _():
            go_left(c, i).wait_recv()

            def add(t):
                total[t] += from_right[c, i, t]

            loop(band, add)

        if c == 0:
            for copy in aux:
                copy.wait_recv()
        for j in range(owned):
            t = o * owned + j
            weight = wts[mine(c), j : j + 1]
            value = weight * (sino[j, mine(c), :].astype(jnp.float32) - total[t])
            band_res[c][i * band + t] = value.astype(jnp.bfloat16)
            t = (1 - o) * owned + j
            rows_here = pl.ds(c * depth, depth)
            weight = mate_wts[rows_here, j : j + 1]
            value = weight * (mate_sino[j, rows_here, :].astype(jnp.float32) - total[t])
            band_res[c][i * band + t] = value.astype(jnp.bfloat16)

        @pl.when(i < n - 1)
        def _():
            share_right(c, i).start()

        @pl.when(i > 0)
        def _():
            share_left(c, i).start()

    def relay(c):
        for d in range(1, n):

            @pl.when(i - d >= 0)
            def _():
                share_right(c, i - d).wait_recv()

                @pl.when(i < n - 1)
                def _():
                    share_right(c, i - d).start()

            @pl.when(i + d <= n - 1)
            def _():
                share_left(c, i + d).wait_recv()

                @pl.when(i > 0)
                def _():
                    share_left(c, i + d).start()

    def give(c):
        return send(picked[c], landed[c], pick_send.at[c], pick_recv.at[c], mate)

    def pick(c):
        def for_mate(k):
            picked[c][k] = band_res[c][mate_idx[k]]

        loop(slots, for_mate)
        give(c).start()

        def for_self(k):
            out_ref[k, mine(c), :] = band_res[c][own_idx[k]]

        loop(slots, for_self)

    def collect(c):
        give(c).wait_recv()

        def copy_in(k):
            out_ref[k, theirs(c), :] = landed[c][k]

        loop(slots, copy_in)

    for step in range(pieces + 3):
        for lag, stage in enumerate((sums, finish, relay, pick)):
            if 0 <= step - lag < pieces:
                stage(step - lag)
    for c in range(pieces):
        collect(c)

    for copy in aux:
        copy.wait_send()
    for c in range(pieces):
        swap(c).wait_send()
        give(c).wait_send()
        for b in range(n):

            @pl.when(b > i)
            def _():
                go_right(c, b).wait_send()

            @pl.when(b < i)
            def _():
                go_left(c, b).wait_send()

            @pl.when(jnp.logical_and(b <= i, i < n - 1))
            def _():
                share_right(c, b).wait_send()

            @pl.when(jnp.logical_and(b >= i, i > 0))
            def _():
                share_left(c, b).wait_send()


def paired_path(volume, projector, slot_ray, slot_pixel, sinogram, weight_index, weight_table):
    n = lax.axis_size("inner")
    slots, per_slot, rows, cols = projector.shape
    patch_tiles, _, slices = volume.shape
    owned = sinogram.shape[0]
    band = 2 * owned
    rays = n * band
    pieces = rows // 2 // PIECE
    depth = PIECE
    order = jnp.arange(slots, dtype=jnp.int32)
    first = jnp.min(
        jnp.where(slot_ray[:, None] == slot_ray[None, :], order[None, :], slots), axis=1
    )
    cell = jnp.min(
        jnp.where(
            jnp.arange(rays, dtype=jnp.int32)[:, None] == slot_ray[None, :], order[None, :], slots
        ),
        axis=1,
    )
    own_idx = jnp.concatenate([slot_ray, cell])
    mate_idx = lax.ppermute(own_idx, "outer", [(0, 1), (1, 0)])
    classes = weight_table.shape[0]
    lookup = weight_index.T[:, :, None] == jnp.arange(classes)[None, None, :]
    weights = jnp.sum(
        jnp.where(lookup, weight_table.astype(jnp.float32)[None, None, :], 0.0), axis=2
    )
    weights = jnp.pad(weights, ((0, 0), (0, -owned % 128)))
    pixel = slot_pixel.reshape(-1)
    block = 4
    tile_spec = pl.BlockSpec((block, per_slot, rows, cols), lambda s, *_: (s, 0, 0, 0))
    volume_spec = pl.BlockSpec(volume.shape, lambda s, *_: (0, 0, 0))
    packed = pl.pallas_call(
        forward_kernel,
        out_shape=jax.ShapeDtypeStruct((slots + 1, rows, slices), jnp.float32),
        grid_spec=pltpu.PrefetchScalarGridSpec(
            num_scalar_prefetch=2,
            grid=(slots // block,),
            in_specs=[volume_spec, tile_spec],
            out_specs=pl.BlockSpec((slots + 1, rows, slices), lambda s, *_: (0, 0, 0)),
        ),
    )(first, pixel, volume, projector)
    f32, bf16 = jnp.float32, jnp.bfloat16
    dma = pltpu.SemaphoreType.DMA
    vmem = pl.BlockSpec(memory_space=pltpu.VMEM)
    smem = pl.BlockSpec(memory_space=pltpu.SMEM)
    scratch = (
        [pltpu.VMEM((slots + 1, depth, slices), f32)] * pieces
        + [pltpu.VMEM((pieces, n, band, depth, slices), f32)] * 3
        + [pltpu.VMEM((band, depth, slices), f32)]
        + [pltpu.VMEM((rays, depth, slices), bf16)] * pieces
        + [pltpu.VMEM((slots, depth, slices), bf16)] * (2 * pieces)
        + [pltpu.VMEM((owned, rows // 2, slices), bf16), pltpu.VMEM((rows // 2, 128), f32)]
        + [dma((pieces,)), dma((pieces,)), dma((2,)), dma((2,))]
        + [dma((pieces, n))] * 6
        + [dma((pieces,)), dma((pieces,))]
    )
    slot_residual = pl.pallas_call(
        functools.partial(exchange_kernel, n, pieces),
        out_shape=jax.ShapeDtypeStruct((slots, rows, slices), bf16),
        in_specs=[smem, smem, vmem, vmem, vmem],
        out_specs=vmem,
        scratch_shapes=scratch,
        compiler_params=pltpu.CompilerParams(collective_id=0, has_side_effects=True),
    )(own_idx, mate_idx, packed, sinogram, weights)
    return pl.pallas_call(
        backward_kernel,
        out_shape=jax.ShapeDtypeStruct(volume.shape, f32),
        grid_spec=pltpu.PrefetchScalarGridSpec(
            num_scalar_prefetch=1,
            grid=(slots // block,),
            in_specs=[
                volume_spec,
                tile_spec,
                pl.BlockSpec((block, rows, slices), lambda s, *_: (s, 0, 0)),
            ],
            out_specs=pl.BlockSpec(volume.shape, lambda s, *_: (0, 0, 0)),
            scratch_shapes=[pltpu.VMEM((patch_tiles, cols, 2 * slices), f32)],
        ),
    )(pixel, volume, projector, slot_residual)


def on_device(volume, projector, slot_ray, slot_pixel, sinogram, weight_index, weight_table):
    inners = lax.axis_size("inner")
    outers = lax.axis_size("outer")
    capacity = 2 * projector.shape[0] // inners
    dense = sinogram.shape[0] * outers <= capacity
    path = paired_path if outers == 2 and dense else general_path
    return path(volume, projector, slot_ray, slot_pixel, sinogram, weight_index, weight_table)


def solution(mesh):
    in_specs = (
        P(("group", "inner", "outer"), None, "cuts"),
        P(("inner", "outer"), None, None, None),
        P(("inner", "outer")),
        P(("inner", "outer"), None),
        P(("group", "inner", "outer"), None, "cuts"),
        P(("group", "inner", "outer"), None),
        P(),
    )
    out_specs = P(("group", "inner", "outer"), None, "cuts")
    return jax.shard_map(
        on_device, mesh=mesh, in_specs=in_specs, out_specs=out_specs, check_vma=False
    )
```

```python
import functools

import jax
import jax.numpy as jnp
from jax import lax
from jax.experimental import pallas as pl
from jax.experimental.pallas import tpu as pltpu
from jax.sharding import PartitionSpec as P

MESH = pl.DeviceIdType.MESH
PIECE = 16
LIMIT = 32000.0


def general_path(volume, projector, slot_ray, slot_pixel, sinogram, weight_index, weight_table):
    inners = lax.axis_size("inner")
    outers = lax.axis_size("outer")
    slot_count = projector.shape[0]
    per_slot = projector.shape[1]
    tile_rows = projector.shape[2]
    tile_cols = projector.shape[3]
    patch_tiles = volume.shape[0]
    slice_count = volume.shape[2]
    owned_rows = sinogram.shape[0]
    band_rows = owned_rows * outers
    capacity = 2 * slot_count // inners
    cell_count = inners * capacity
    target = slot_ray // band_rows
    offset = slot_ray % band_rows
    same_target = target[:, None] == target[None, :]
    earlier = jnp.arange(slot_count)[:, None] > jnp.arange(slot_count)[None, :]
    slot_rank = jnp.sum(jnp.logical_and(same_target, earlier), axis=1)
    position = target * capacity + slot_rank
    partial_value = jnp.zeros((slot_count, tile_rows, slice_count), jnp.float32)
    for column in range(per_slot):
        pixels = volume[slot_pixel[:, column]]
        partial_value = partial_value + jnp.einsum(
            "srp,spc->src", projector[:, column], pixels, preferred_element_type=jnp.float32
        )
    outgoing = (
        jnp.zeros((cell_count, tile_rows, slice_count), jnp.float32).at[position].set(partial_value)
    )
    labels = jnp.full((cell_count,), -1.0, jnp.float32).at[position].set(offset.astype(jnp.float32))
    arrived, arrived_rows = (
        lax.all_to_all(
            outgoing.reshape(inners, capacity, tile_rows, slice_count),
            "inner",
            split_axis=0,
            concat_axis=0,
            tiled=True,
        ),
        lax.all_to_all(
            labels.reshape(inners, capacity), "inner", split_axis=0, concat_axis=0, tiled=True
        ),
    )
    selector = (
        jnp.arange(band_rows, dtype=jnp.float32)[:, None] == arrived_rows.reshape(1, cell_count)
    ).astype(jnp.float32)
    block_sums = jnp.dot(
        selector,
        arrived.reshape(cell_count, tile_rows * slice_count),
        precision=lax.Precision.HIGHEST,
    ).reshape(band_rows, tile_rows, slice_count)
    classes = weight_table.shape[0]
    lookup = weight_index[:, :, None] == jnp.arange(classes)[None, None, :]
    weights = jnp.sum(
        jnp.where(lookup, weight_table[None, None, :], jnp.zeros((), weight_table.dtype)), axis=2
    )
    own_sums = lax.psum_scatter(block_sums, "outer", scatter_dimension=0, tiled=True)
    own_residual = (
        weights.astype(jnp.float32)[:, :, None] * (sinogram.astype(jnp.float32) - own_sums)
    ).astype(jnp.bfloat16)
    residual = lax.all_gather(own_residual, "outer", axis=0, tiled=True)
    picked = jnp.dot(
        selector.T.astype(jnp.bfloat16),
        residual.reshape(band_rows, tile_rows * slice_count),
        preferred_element_type=jnp.float32,
    ).astype(jnp.bfloat16)
    returned = lax.all_to_all(
        picked.reshape(inners, capacity, tile_rows, slice_count),
        "inner",
        split_axis=0,
        concat_axis=0,
        tiled=True,
    )
    slot_residual = returned.reshape(cell_count, tile_rows, slice_count)[position]
    owners = jnp.arange(patch_tiles)
    backward = jnp.zeros((patch_tiles, tile_cols, slice_count), jnp.float32)
    column_sum = jnp.zeros((patch_tiles, tile_cols), jnp.float32)
    for column in range(per_slot):
        member = (owners[:, None] == slot_pixel[None, :, column]).astype(jnp.float32)
        spread = jnp.einsum(
            "srp,src->spc", projector[:, column], slot_residual, preferred_element_type=jnp.float32
        )
        backward = backward + jnp.einsum(
            "ts,spc->tpc", member, spread, precision=lax.Precision.HIGHEST
        )
        column_sum = column_sum + jnp.dot(
            member,
            jnp.sum(projector[:, column], axis=1, dtype=jnp.float32),
            precision=lax.Precision.HIGHEST,
        )
    return volume.astype(jnp.float32) + backward / column_sum[:, :, None]


def exponent_of(largest):
    top = jnp.max(largest, axis=0, keepdims=True)
    exponent = jnp.ceil(jnp.log2(jnp.maximum(top, 1e-20) * (1.0 / LIMIT)))
    return jnp.broadcast_to(exponent, largest.shape)


def encode(value, inverse):
    return jnp.round(value * inverse).astype(jnp.int32).astype(jnp.int16)


def decode(coded):
    return coded.astype(jnp.int32).astype(jnp.float32)


def forward_kernel(first_ref, pixel_ref, volume_ref, projector_ref, coded_ref, packed_ref):
    step = pl.program_id(0)
    block, per_slot = projector_ref.shape[:2]
    slots, rows, slices = packed_ref.shape

    @pl.when(step == 0)
    def _():
        packed_ref[...] = jnp.zeros_like(packed_ref)

    for j in range(block):
        s = step * block + j
        pixels = jnp.concatenate(
            [volume_ref[pixel_ref[s * per_slot + g]] for g in range(per_slot)], axis=0
        )
        tiles = jnp.concatenate([projector_ref[j, g] for g in range(per_slot)], axis=1)
        packed_ref[first_ref[s]] += jnp.dot(tiles, pixels, preferred_element_type=jnp.float32)

    @pl.when(step == pl.num_programs(0) - 1)
    def _():
        largest = jnp.zeros((PIECE, slices), jnp.float32)
        for s in range(slots):
            for r in range(0, rows, PIECE):
                largest = jnp.maximum(largest, jnp.abs(packed_ref[s, r : r + PIECE]))
        exponent = exponent_of(largest)
        inverse = jnp.exp2(-exponent)
        for s in range(slots):
            for r in range(0, rows, PIECE):
                coded_ref[s, r : r + PIECE] = encode(packed_ref[s, r : r + PIECE], inverse)
        for r in range(0, rows, PIECE):
            coded_ref[slots, r : r + PIECE] = jnp.zeros((PIECE, slices), jnp.int16)
            coded_ref[slots + 1, r : r + PIECE] = exponent.astype(jnp.int32).astype(jnp.int16)


def backward_kernel(pixel_ref, volume_ref, projector_ref, residual_ref, out_ref, acc_ref):
    step = pl.program_id(0)
    block, per_slot, rows, cols = projector_ref.shape
    slices = residual_ref.shape[-1]

    @pl.when(step == 0)
    def _():
        acc_ref[...] = jnp.zeros_like(acc_ref)

    ones = jnp.ones((rows, slices), jnp.bfloat16)
    for j in range(block):
        s = step * block + j
        wide = jnp.concatenate([residual_ref[j], ones], axis=1)
        tiles = jnp.concatenate([projector_ref[j, g] for g in range(per_slot)], axis=1)
        spread = lax.dot_general(
            tiles, wide, (((0,), (0,)), ((), ())), preferred_element_type=jnp.float32
        )
        for g in range(per_slot):
            acc_ref[pixel_ref[s * per_slot + g]] += spread[g * cols : (g + 1) * cols]

    @pl.when(step == pl.num_programs(0) - 1)
    def _():
        out_ref[...] = (
            volume_ref[...].astype(jnp.float32) + acc_ref[:, :, :slices] / acc_ref[:, :, slices:]
        )


def exchange_kernel(n, pieces, own_idx, mate_idx, packed, sino, wts, out_ref, *scratch):
    take = iter(scratch)
    mate_part = [next(take) for _ in range(pieces)]
    from_left, from_right, going, total = (next(take) for _ in range(4))
    band_res = [next(take) for _ in range(pieces)]
    picked = [next(take) for _ in range(pieces)]
    landed = [next(take) for _ in range(pieces)]
    mate_sino, mate_wts = next(take), next(take)
    x_send, x_recv, aux_send, aux_recv, sum_send, left_recv, right_recv = (
        next(take) for _ in range(7)
    )
    out_right, out_left, res_recv, pick_send, pick_recv = (next(take) for _ in range(5))

    slots, rows, slices = out_ref.shape
    owned = sino.shape[0]
    band = 2 * owned
    half = rows // 2
    depth = half // pieces
    i = lax.axis_index("inner")
    o = lax.axis_index("outer")
    mate = {"outer": 1 - o}
    right = {"inner": i + 1}
    left = {"inner": i - 1}

    def send(src, dst, ssem, rsem, device):
        return pltpu.make_async_remote_copy(
            src_ref=src, dst_ref=dst, send_sem=ssem, recv_sem=rsem, device_id=device,
            device_id_type=MESH,
        )

    barrier = pltpu.get_barrier_semaphore()
    pl.semaphore_signal(barrier, inc=1, device_id=mate, device_id_type=MESH)

    @pl.when(i > 0)
    def _():
        pl.semaphore_signal(barrier, inc=1, device_id=left, device_id_type=MESH)

    @pl.when(i < n - 1)
    def _():
        pl.semaphore_signal(barrier, inc=1, device_id=right, device_id_type=MESH)

    pl.semaphore_wait(barrier, jnp.where(i > 0, 2, 1) + jnp.where(i < n - 1, 1, 0))

    def mine(c):
        return pl.ds(pl.multiple_of(o * half + c * depth, depth), depth)

    def theirs(c):
        return pl.ds(pl.multiple_of((1 - o) * half + c * depth, depth), depth)

    def swap(c):
        return send(
            packed.at[:, theirs(c)],
            mate_part[c],
            x_send.at[c],
            x_recv.at[c],
            mate,
        )

    other_half = pl.ds(pl.multiple_of((1 - o) * half, half), half)
    aux = [
        send(sino.at[:, other_half], mate_sino, aux_send.at[0], aux_recv.at[0], mate),
        send(wts.at[other_half], mate_wts, aux_send.at[1], aux_recv.at[1], mate),
    ]
    for c in range(pieces):
        swap(c).start()
        if c == min(1, pieces - 1):
            for copy in aux:
                copy.start()
    def local_scales(c):
        return (
            jnp.exp2(decode(packed[slots + 1, mine(c), :])),
            jnp.exp2(decode(mate_part[c][slots + 1])),
        )

    def local(c, r, scales):
        return (
            decode(packed[own_idx[slots + r], mine(c), :]) * scales[0]
            + decode(mate_part[c][mate_idx[slots + r]]) * scales[1]
        )

    def loop(count, body):
        def step(t, carry):
            body(t)
            return carry

        lax.fori_loop(0, count, step, 0, unroll=4)

    def go_right(c, b):
        return send(
            going.at[c, b], from_left.at[c, b], sum_send.at[c, b], left_recv.at[c, b], right
        )

    def go_left(c, b):
        return send(
            going.at[c, b], from_right.at[c, b], sum_send.at[c, b], right_recv.at[c, b], left
        )

    def sums(c):
        swap(c).wait_recv()

        def one(b, to_right):
            scales = local_scales(c)

            def fill(t):
                total[t] = local(c, b * band + t, scales)

            loop(band, fill)
            inner_side = i > 0 if to_right else i < n - 1
            arrived = from_left if to_right else from_right

            @pl.when(inner_side)
            def _():
                (go_right if to_right else go_left)(c, b).wait_recv()

                scale = jnp.exp2(decode(arrived[c, b, band]))

                def add(t):
                    total[t] += decode(arrived[c, b, t]) * scale

                loop(band, add)

            def widest(t, largest):
                return jnp.maximum(largest, jnp.abs(total[t]))

            exponent = exponent_of(
                lax.fori_loop(0, band, widest, jnp.zeros((depth, slices), jnp.float32), unroll=4)
            )
            inverse = jnp.exp2(-exponent)

            def pack(t):
                going[c, b, t] = encode(total[t], inverse)

            loop(band, pack)
            going[c, b, band] = exponent.astype(jnp.int32).astype(jnp.int16)
            (go_right if to_right else go_left)(c, b).start()

        for far in range(n - 1):
            b = n - 1 - far
            pl.when(b > i)(functools.partial(one, b, True))
            pl.when(far < i)(functools.partial(one, far, False))

    def share_right(c, b):
        part = band_res[c].at[pl.ds(pl.multiple_of(b * band, band), band)]
        return send(part, part, out_right.at[c, b], res_recv.at[c, b], right)

    def share_left(c, b):
        part = band_res[c].at[pl.ds(pl.multiple_of(b * band, band), band)]
        return send(part, part, out_left.at[c, b], res_recv.at[c, b], left)

    def finish(c):
        scales = local_scales(c)

        def start_total(t):
            total[t] = local(c, i * band + t, scales)

        loop(band, start_total)

        @pl.when(i > 0)
        def _():
            go_right(c, i).wait_recv()

            scale = jnp.exp2(decode(from_left[c, i, band]))

            def add(t):
                total[t] += decode(from_left[c, i, t]) * scale

            loop(band, add)

        @pl.when(i < n - 1)
        def _():
            go_left(c, i).wait_recv()

            scale = jnp.exp2(decode(from_right[c, i, band]))

            def add(t):
                total[t] += decode(from_right[c, i, t]) * scale

            loop(band, add)

        if c == 0:
            for copy in aux:
                copy.wait_recv()
        for j in range(owned):
            t = o * owned + j
            weight = wts[mine(c), j : j + 1]
            value = weight * (sino[j, mine(c), :].astype(jnp.float32) - total[t])
            band_res[c][i * band + t] = value.astype(jnp.bfloat16)
            t = (1 - o) * owned + j
            rows_here = pl.ds(c * depth, depth)
            weight = mate_wts[rows_here, j : j + 1]
            value = weight * (mate_sino[j, rows_here, :].astype(jnp.float32) - total[t])
            band_res[c][i * band + t] = value.astype(jnp.bfloat16)

        @pl.when(i < n - 1)
        def _():
            share_right(c, i).start()

        @pl.when(i > 0)
        def _():
            share_left(c, i).start()

    def relay(c):
        for d in range(1, n):

            @pl.when(i - d >= 0)
            def _():
                share_right(c, i - d).wait_recv()

                @pl.when(i < n - 1)
                def _():
                    share_right(c, i - d).start()

            @pl.when(i + d <= n - 1)
            def _():
                share_left(c, i + d).wait_recv()

                @pl.when(i > 0)
                def _():
                    share_left(c, i + d).start()

    def give(c):
        return send(picked[c], landed[c], pick_send.at[c], pick_recv.at[c], mate)

    def pick(c):
        def for_mate(k):
            picked[c][k] = band_res[c][mate_idx[k]]

        loop(slots, for_mate)
        give(c).start()

        def for_self(k):
            out_ref[k, mine(c), :] = band_res[c][own_idx[k]]

        loop(slots, for_self)

    def collect(c):
        give(c).wait_recv()

        def copy_in(k):
            out_ref[k, theirs(c), :] = landed[c][k]

        loop(slots, copy_in)

    for step in range(pieces + 3):
        for lag, stage in enumerate((sums, finish, relay, pick)):
            if 0 <= step - lag < pieces:
                stage(step - lag)
    for c in range(pieces):
        collect(c)

    for copy in aux:
        copy.wait_send()
    for c in range(pieces):
        swap(c).wait_send()
        give(c).wait_send()
        for b in range(n):

            @pl.when(b > i)
            def _():
                go_right(c, b).wait_send()

            @pl.when(b < i)
            def _():
                go_left(c, b).wait_send()

            @pl.when(jnp.logical_and(b <= i, i < n - 1))
            def _():
                share_right(c, b).wait_send()

            @pl.when(jnp.logical_and(b >= i, i > 0))
            def _():
                share_left(c, b).wait_send()


def paired_path(volume, projector, slot_ray, slot_pixel, sinogram, weight_index, weight_table):
    n = lax.axis_size("inner")
    slots, per_slot, rows, cols = projector.shape
    patch_tiles, _, slices = volume.shape
    owned = sinogram.shape[0]
    band = 2 * owned
    rays = n * band
    pieces = rows // 2 // PIECE
    depth = PIECE
    order = jnp.arange(slots, dtype=jnp.int32)
    first = jnp.min(
        jnp.where(slot_ray[:, None] == slot_ray[None, :], order[None, :], slots), axis=1
    )
    cell = jnp.min(
        jnp.where(
            jnp.arange(rays, dtype=jnp.int32)[:, None] == slot_ray[None, :], order[None, :], slots
        ),
        axis=1,
    )
    own_idx = jnp.concatenate([slot_ray, cell])
    mate_idx = lax.ppermute(own_idx, "outer", [(0, 1), (1, 0)])
    classes = weight_table.shape[0]
    lookup = weight_index.T[:, :, None] == jnp.arange(classes)[None, None, :]
    weights = jnp.sum(
        jnp.where(lookup, weight_table.astype(jnp.float32)[None, None, :], 0.0), axis=2
    )
    weights = jnp.pad(weights, ((0, 0), (0, -owned % 128)))
    pixel = slot_pixel.reshape(-1)
    block = 4
    tile_spec = pl.BlockSpec((block, per_slot, rows, cols), lambda s, *_: (s, 0, 0, 0))
    volume_spec = pl.BlockSpec(volume.shape, lambda s, *_: (0, 0, 0))
    packed = pl.pallas_call(
        forward_kernel,
        out_shape=jax.ShapeDtypeStruct((slots + 2, rows, slices), jnp.int16),
        grid_spec=pltpu.PrefetchScalarGridSpec(
            num_scalar_prefetch=2,
            grid=(slots // block,),
            in_specs=[volume_spec, tile_spec],
            out_specs=pl.BlockSpec((slots + 2, rows, slices), lambda s, *_: (0, 0, 0)),
            scratch_shapes=[pltpu.VMEM((slots, rows, slices), jnp.float32)],
        ),
    )(first, pixel, volume, projector)
    f32, bf16 = jnp.float32, jnp.bfloat16
    dma = pltpu.SemaphoreType.DMA
    vmem = pl.BlockSpec(memory_space=pltpu.VMEM)
    smem = pl.BlockSpec(memory_space=pltpu.SMEM)
    scratch = (
        [pltpu.VMEM((slots + 2, depth, slices), jnp.int16)] * pieces
        + [pltpu.VMEM((pieces, n, band + 1, depth, slices), jnp.int16)] * 3
        + [pltpu.VMEM((band, depth, slices), f32)]
        + [pltpu.VMEM((rays, depth, slices), bf16)] * pieces
        + [pltpu.VMEM((slots, depth, slices), bf16)] * (2 * pieces)
        + [pltpu.VMEM((owned, rows // 2, slices), bf16), pltpu.VMEM((rows // 2, 128), f32)]
        + [dma((pieces,)), dma((pieces,)), dma((2,)), dma((2,))]
        + [dma((pieces, n))] * 6
        + [dma((pieces,)), dma((pieces,))]
    )
    slot_residual = pl.pallas_call(
        functools.partial(exchange_kernel, n, pieces),
        out_shape=jax.ShapeDtypeStruct((slots, rows, slices), bf16),
        in_specs=[smem, smem, vmem, vmem, vmem],
        out_specs=vmem,
        scratch_shapes=scratch,
        compiler_params=pltpu.CompilerParams(collective_id=0, has_side_effects=True),
    )(own_idx, mate_idx, packed, sinogram, weights)
    return pl.pallas_call(
        backward_kernel,
        out_shape=jax.ShapeDtypeStruct(volume.shape, f32),
        grid_spec=pltpu.PrefetchScalarGridSpec(
            num_scalar_prefetch=1,
            grid=(slots // block,),
            in_specs=[
                volume_spec,
                tile_spec,
                pl.BlockSpec((block, rows, slices), lambda s, *_: (s, 0, 0)),
            ],
            out_specs=pl.BlockSpec(volume.shape, lambda s, *_: (0, 0, 0)),
            scratch_shapes=[pltpu.VMEM((patch_tiles, cols, 2 * slices), f32)],
        ),
    )(pixel, volume, projector, slot_residual)


def on_device(volume, projector, slot_ray, slot_pixel, sinogram, weight_index, weight_table):
    inners = lax.axis_size("inner")
    outers = lax.axis_size("outer")
    capacity = 2 * projector.shape[0] // inners
    dense = sinogram.shape[0] * outers <= capacity
    path = paired_path if outers == 2 and dense else general_path
    return path(volume, projector, slot_ray, slot_pixel, sinogram, weight_index, weight_table)


def solution(mesh):
    in_specs = (
        P(("group", "inner", "outer"), None, "cuts"),
        P(("inner", "outer"), None, None, None),
        P(("inner", "outer")),
        P(("inner", "outer"), None),
        P(("group", "inner", "outer"), None, "cuts"),
        P(("group", "inner", "outer"), None),
        P(),
    )
    out_specs = P(("group", "inner", "outer"), None, "cuts")
    return jax.shard_map(
        on_device, mesh=mesh, in_specs=in_specs, out_specs=out_specs, check_vma=False
    )
```

```python
import functools

import jax
import jax.numpy as jnp
from jax import lax
from jax.experimental import pallas as pl
from jax.experimental.pallas import tpu as pltpu
from jax.sharding import PartitionSpec as P

MESH = pl.DeviceIdType.MESH
PIECE = 16
LIMIT = 32000.0


def general_path(volume, projector, slot_ray, slot_pixel, sinogram, weight_index, weight_table):
    inners = lax.axis_size("inner")
    outers = lax.axis_size("outer")
    slot_count = projector.shape[0]
    per_slot = projector.shape[1]
    tile_rows = projector.shape[2]
    tile_cols = projector.shape[3]
    patch_tiles = volume.shape[0]
    slice_count = volume.shape[2]
    owned_rows = sinogram.shape[0]
    band_rows = owned_rows * outers
    capacity = 2 * slot_count // inners
    cell_count = inners * capacity
    target = slot_ray // band_rows
    offset = slot_ray % band_rows
    same_target = target[:, None] == target[None, :]
    earlier = jnp.arange(slot_count)[:, None] > jnp.arange(slot_count)[None, :]
    slot_rank = jnp.sum(jnp.logical_and(same_target, earlier), axis=1)
    position = target * capacity + slot_rank
    partial_value = jnp.zeros((slot_count, tile_rows, slice_count), jnp.float32)
    for column in range(per_slot):
        pixels = volume[slot_pixel[:, column]]
        partial_value = partial_value + jnp.einsum(
            "srp,spc->src", projector[:, column], pixels, preferred_element_type=jnp.float32
        )
    outgoing = (
        jnp.zeros((cell_count, tile_rows, slice_count), jnp.float32).at[position].set(partial_value)
    )
    labels = jnp.full((cell_count,), -1.0, jnp.float32).at[position].set(offset.astype(jnp.float32))
    arrived, arrived_rows = (
        lax.all_to_all(
            outgoing.reshape(inners, capacity, tile_rows, slice_count),
            "inner",
            split_axis=0,
            concat_axis=0,
            tiled=True,
        ),
        lax.all_to_all(
            labels.reshape(inners, capacity), "inner", split_axis=0, concat_axis=0, tiled=True
        ),
    )
    selector = (
        jnp.arange(band_rows, dtype=jnp.float32)[:, None] == arrived_rows.reshape(1, cell_count)
    ).astype(jnp.float32)
    block_sums = jnp.dot(
        selector,
        arrived.reshape(cell_count, tile_rows * slice_count),
        precision=lax.Precision.HIGHEST,
    ).reshape(band_rows, tile_rows, slice_count)
    classes = weight_table.shape[0]
    lookup = weight_index[:, :, None] == jnp.arange(classes)[None, None, :]
    weights = jnp.sum(
        jnp.where(lookup, weight_table[None, None, :], jnp.zeros((), weight_table.dtype)), axis=2
    )
    own_sums = lax.psum_scatter(block_sums, "outer", scatter_dimension=0, tiled=True)
    own_residual = (
        weights.astype(jnp.float32)[:, :, None] * (sinogram.astype(jnp.float32) - own_sums)
    ).astype(jnp.bfloat16)
    residual = lax.all_gather(own_residual, "outer", axis=0, tiled=True)
    picked = jnp.dot(
        selector.T.astype(jnp.bfloat16),
        residual.reshape(band_rows, tile_rows * slice_count),
        preferred_element_type=jnp.float32,
    ).astype(jnp.bfloat16)
    returned = lax.all_to_all(
        picked.reshape(inners, capacity, tile_rows, slice_count),
        "inner",
        split_axis=0,
        concat_axis=0,
        tiled=True,
    )
    slot_residual = returned.reshape(cell_count, tile_rows, slice_count)[position]
    owners = jnp.arange(patch_tiles)
    backward = jnp.zeros((patch_tiles, tile_cols, slice_count), jnp.float32)
    column_sum = jnp.zeros((patch_tiles, tile_cols), jnp.float32)
    for column in range(per_slot):
        member = (owners[:, None] == slot_pixel[None, :, column]).astype(jnp.float32)
        spread = jnp.einsum(
            "srp,src->spc", projector[:, column], slot_residual, preferred_element_type=jnp.float32
        )
        backward = backward + jnp.einsum(
            "ts,spc->tpc", member, spread, precision=lax.Precision.HIGHEST
        )
        column_sum = column_sum + jnp.dot(
            member,
            jnp.sum(projector[:, column], axis=1, dtype=jnp.float32),
            precision=lax.Precision.HIGHEST,
        )
    return volume.astype(jnp.float32) + backward / column_sum[:, :, None]


def exponent_of(largest):
    top = jnp.max(largest, axis=0, keepdims=True)
    exponent = jnp.ceil(jnp.log2(jnp.maximum(top, 1e-20) * (1.0 / LIMIT)))
    return jnp.broadcast_to(exponent, largest.shape)


def encode(value, inverse):
    return jnp.round(value * inverse).astype(jnp.int32).astype(jnp.int16)


def decode(coded):
    return coded.astype(jnp.int32).astype(jnp.float32)


def forward_kernel(first_ref, pixel_ref, volume_ref, projector_ref, coded_ref, packed_ref):
    step = pl.program_id(0)
    block, per_slot = projector_ref.shape[:2]
    slots, rows, slices = packed_ref.shape

    @pl.when(step == 0)
    def _():
        packed_ref[...] = jnp.zeros_like(packed_ref)

    for j in range(block):
        s = step * block + j
        pixels = jnp.concatenate(
            [volume_ref[pixel_ref[s * per_slot + g]] for g in range(per_slot)], axis=0
        )
        tiles = jnp.concatenate([projector_ref[j, g] for g in range(per_slot)], axis=1)
        packed_ref[first_ref[s]] += jnp.dot(tiles, pixels, preferred_element_type=jnp.float32)

    @pl.when(step == pl.num_programs(0) - 1)
    def _():
        largest = jnp.zeros((PIECE, slices), jnp.float32)
        for s in range(slots):
            for r in range(0, rows, PIECE):
                largest = jnp.maximum(largest, jnp.abs(packed_ref[s, r : r + PIECE]))
        exponent = exponent_of(largest)
        inverse = jnp.exp2(-exponent)
        for s in range(slots):
            for r in range(0, rows, PIECE):
                coded_ref[s, r : r + PIECE] = encode(packed_ref[s, r : r + PIECE], inverse)
        for r in range(0, rows, PIECE):
            coded_ref[slots, r : r + PIECE] = jnp.zeros((PIECE, slices), jnp.int16)
            coded_ref[slots + 1, r : r + PIECE] = exponent.astype(jnp.int32).astype(jnp.int16)


def backward_kernel(pixel_ref, volume_ref, projector_ref, residual_ref, out_ref, acc_ref):
    step = pl.program_id(0)
    block, per_slot, rows, cols = projector_ref.shape
    slices = residual_ref.shape[-1]

    @pl.when(step == 0)
    def _():
        acc_ref[...] = jnp.zeros_like(acc_ref)

    ones = jnp.ones((rows, slices), jnp.bfloat16)
    for j in range(block):
        s = step * block + j
        wide = jnp.concatenate([residual_ref[j], ones], axis=1)
        tiles = jnp.concatenate([projector_ref[j, g] for g in range(per_slot)], axis=1)
        spread = lax.dot_general(
            tiles, wide, (((0,), (0,)), ((), ())), preferred_element_type=jnp.float32
        )
        for g in range(per_slot):
            acc_ref[pixel_ref[s * per_slot + g]] += spread[g * cols : (g + 1) * cols]

    @pl.when(step == pl.num_programs(0) - 1)
    def _():
        out_ref[...] = (
            volume_ref[...].astype(jnp.float32) + acc_ref[:, :, :slices] / acc_ref[:, :, slices:]
        )


def exchange_kernel(n, pieces, own_idx, mate_idx, packed, sino, wts, out_ref, *scratch):
    take = iter(scratch)
    mate_part = [next(take) for _ in range(pieces)]
    from_left, from_right, going, dense = (next(take) for _ in range(4))
    band_res = [next(take) for _ in range(pieces)]
    picked = [next(take) for _ in range(pieces)]
    landed = [next(take) for _ in range(pieces)]
    mate_sino, mate_wts = next(take), next(take)
    x_send, x_recv, aux_send, aux_recv, sum_send, left_recv, right_recv = (
        next(take) for _ in range(7)
    )
    out_right, out_left, res_recv, pick_send, pick_recv = (next(take) for _ in range(5))

    slots, rows, slices = out_ref.shape
    owned = sino.shape[0]
    band = 2 * owned
    half = rows // 2
    depth = half // pieces
    i = lax.axis_index("inner")
    o = lax.axis_index("outer")
    mate = {"outer": 1 - o}
    right = {"inner": i + 1}
    left = {"inner": i - 1}

    def send(src, dst, ssem, rsem, device):
        return pltpu.make_async_remote_copy(
            src_ref=src, dst_ref=dst, send_sem=ssem, recv_sem=rsem, device_id=device,
            device_id_type=MESH,
        )

    barrier = pltpu.get_barrier_semaphore()
    pl.semaphore_signal(barrier, inc=1, device_id=mate, device_id_type=MESH)

    @pl.when(i > 0)
    def _():
        pl.semaphore_signal(barrier, inc=1, device_id=left, device_id_type=MESH)

    @pl.when(i < n - 1)
    def _():
        pl.semaphore_signal(barrier, inc=1, device_id=right, device_id_type=MESH)

    pl.semaphore_wait(barrier, jnp.where(i > 0, 2, 1) + jnp.where(i < n - 1, 1, 0))

    def mine(c):
        return pl.ds(pl.multiple_of(o * half + c * depth, depth), depth)

    def theirs(c):
        return pl.ds(pl.multiple_of((1 - o) * half + c * depth, depth), depth)

    def swap(c):
        return send(
            packed.at[:, theirs(c)],
            mate_part[c],
            x_send.at[c],
            x_recv.at[c],
            mate,
        )

    other_half = pl.ds(pl.multiple_of((1 - o) * half, half), half)
    aux = [
        send(sino.at[:, other_half], mate_sino, aux_send.at[0], aux_recv.at[0], mate),
        send(wts.at[other_half], mate_wts, aux_send.at[1], aux_recv.at[1], mate),
    ]
    for c in range(pieces):
        swap(c).start()
        if c == min(1, pieces - 1):
            for copy in aux:
                copy.start()
    def local_scales(c):
        return (
            jnp.exp2(decode(packed[slots + 1, mine(c), :])),
            jnp.exp2(decode(mate_part[c][slots + 1])),
        )

    def local(c, r, scales):
        return (
            decode(packed[own_idx[slots + r], mine(c), :]) * scales[0]
            + decode(mate_part[c][mate_idx[slots + r]]) * scales[1]
        )

    def loop(count, body):
        def step(t, carry):
            body(t)
            return carry

        lax.fori_loop(0, count, step, 0, unroll=4)

    def go_right(c, b):
        return send(
            going.at[c, b], from_left.at[c, b], sum_send.at[c, b], left_recv.at[c, b], right
        )

    def go_left(c, b):
        return send(
            going.at[c, b], from_right.at[c, b], sum_send.at[c, b], right_recv.at[c, b], left
        )

    def gather(c):
        swap(c).wait_recv()
        scales = local_scales(c)

        def fill(r):
            dense[c, r] = local(c, r, scales)

        loop(n * band, fill)

    def hop(c, b, to_right):
        copy = (go_right if to_right else go_left)(c, b)
        arrived = from_left if to_right else from_right

        def widest(t, largest):
            return jnp.maximum(largest, jnp.abs(dense[c, b * band + t]))

        @pl.when(i > 0 if to_right else i < n - 1)
        def _():
            copy.wait_recv()
            scale = jnp.exp2(decode(arrived[c, b, band]))

            def add(t):
                dense[c, b * band + t] += decode(arrived[c, b, t]) * scale

            loop(band, add)

        exponent = exponent_of(
            lax.fori_loop(0, band, widest, jnp.zeros((depth, slices), jnp.float32), unroll=4)
        )
        inverse = jnp.exp2(-exponent)

        def pack(t):
            going[c, b, t] = encode(dense[c, b * band + t], inverse)

        loop(band, pack)
        going[c, b, band] = exponent.astype(jnp.int32).astype(jnp.int16)
        copy.start()

    def sums(step):
        def rightward(far, carry):
            hop(step - i, n - 1 - far, True)
            return carry

        def leftward(far, carry):
            hop(step - (n - 1 - i), far, False)
            return carry

        @pl.when(jnp.logical_and(step >= i, step - i < pieces))
        def _():
            lax.fori_loop(0, n - 1 - i, rightward, 0)

        @pl.when(jnp.logical_and(step >= n - 1 - i, step - (n - 1 - i) < pieces))
        def _():
            lax.fori_loop(0, i, leftward, 0)

    def share_right(c, b):
        part = band_res[c].at[pl.ds(pl.multiple_of(b * band, band), band)]
        return send(part, part, out_right.at[c, b], res_recv.at[c, b], right)

    def share_left(c, b):
        part = band_res[c].at[pl.ds(pl.multiple_of(b * band, band), band)]
        return send(part, part, out_left.at[c, b], res_recv.at[c, b], left)

    def finish(c):
        @pl.when(i > 0)
        def _():
            go_right(c, i).wait_recv()

            scale = jnp.exp2(decode(from_left[c, i, band]))

            def add(t):
                dense[c, i * band + t] += decode(from_left[c, i, t]) * scale

            loop(band, add)

        @pl.when(i < n - 1)
        def _():
            go_left(c, i).wait_recv()

            scale = jnp.exp2(decode(from_right[c, i, band]))

            def add(t):
                dense[c, i * band + t] += decode(from_right[c, i, t]) * scale

            loop(band, add)

        if c == 0:
            for copy in aux:
                copy.wait_recv()
        for j in range(owned):
            t = o * owned + j
            weight = wts[mine(c), j : j + 1]
            value = weight * (sino[j, mine(c), :].astype(jnp.float32) - dense[c, i * band + t])
            band_res[c][i * band + t] = value.astype(jnp.bfloat16)
            t = (1 - o) * owned + j
            rows_here = pl.ds(c * depth, depth)
            weight = mate_wts[rows_here, j : j + 1]
            value = weight * (mate_sino[j, rows_here, :].astype(jnp.float32) - dense[c, i * band + t])
            band_res[c][i * band + t] = value.astype(jnp.bfloat16)

        @pl.when(i < n - 1)
        def _():
            share_right(c, i).start()

        @pl.when(i > 0)
        def _():
            share_left(c, i).start()

    def relay(c, d):
        @pl.when(i - d >= 0)
        def _():
            share_right(c, i - d).wait_recv()

            @pl.when(i < n - 1)
            def _():
                share_right(c, i - d).start()

        @pl.when(i + d <= n - 1)
        def _():
            share_left(c, i + d).wait_recv()

            @pl.when(i > 0)
            def _():
                share_left(c, i + d).start()

    def give(c):
        return send(picked[c], landed[c], pick_send.at[c], pick_recv.at[c], mate)

    def pick(c):
        def for_mate(k):
            picked[c][k] = band_res[c][mate_idx[k]]

        loop(slots, for_mate)
        give(c).start()

        def for_self(k):
            out_ref[k, mine(c), :] = band_res[c][own_idx[k]]

        loop(slots, for_self)

    def collect(c):
        give(c).wait_recv()

        def copy_in(k):
            out_ref[k, theirs(c), :] = landed[c][k]

        loop(slots, copy_in)

    for step in range(pieces + 2 * (n - 1)):
        if step < pieces:
            gather(step)
        if step < pieces + n - 1:
            sums(step)
        for d in range(n):
            c = step - (n - 1) - d
            if 0 <= c < pieces:
                if d == 0:
                    finish(c)
                else:
                    relay(c, d)
                if d == n - 1:
                    pick(c)
    for c in range(pieces):
        collect(c)

    for copy in aux:
        copy.wait_send()
    for c in range(pieces):
        swap(c).wait_send()
        give(c).wait_send()
        for b in range(n):

            @pl.when(b > i)
            def _():
                go_right(c, b).wait_send()

            @pl.when(b < i)
            def _():
                go_left(c, b).wait_send()

            @pl.when(jnp.logical_and(b <= i, i < n - 1))
            def _():
                share_right(c, b).wait_send()

            @pl.when(jnp.logical_and(b >= i, i > 0))
            def _():
                share_left(c, b).wait_send()


def paired_path(volume, projector, slot_ray, slot_pixel, sinogram, weight_index, weight_table):
    n = lax.axis_size("inner")
    slots, per_slot, rows, cols = projector.shape
    patch_tiles, _, slices = volume.shape
    owned = sinogram.shape[0]
    band = 2 * owned
    rays = n * band
    pieces = rows // 2 // PIECE
    depth = PIECE
    order = jnp.arange(slots, dtype=jnp.int32)
    first = jnp.min(
        jnp.where(slot_ray[:, None] == slot_ray[None, :], order[None, :], slots), axis=1
    )
    cell = jnp.min(
        jnp.where(
            jnp.arange(rays, dtype=jnp.int32)[:, None] == slot_ray[None, :], order[None, :], slots
        ),
        axis=1,
    )
    own_idx = jnp.concatenate([slot_ray, cell])
    mate_idx = lax.ppermute(own_idx, "outer", [(0, 1), (1, 0)])
    classes = weight_table.shape[0]
    lookup = weight_index.T[:, :, None] == jnp.arange(classes)[None, None, :]
    weights = jnp.sum(
        jnp.where(lookup, weight_table.astype(jnp.float32)[None, None, :], 0.0), axis=2
    )
    weights = jnp.pad(weights, ((0, 0), (0, -owned % 128)))
    pixel = slot_pixel.reshape(-1)
    block = 4
    tile_spec = pl.BlockSpec((block, per_slot, rows, cols), lambda s, *_: (s, 0, 0, 0))
    volume_spec = pl.BlockSpec(volume.shape, lambda s, *_: (0, 0, 0))
    packed = pl.pallas_call(
        forward_kernel,
        out_shape=jax.ShapeDtypeStruct((slots + 2, rows, slices), jnp.int16),
        grid_spec=pltpu.PrefetchScalarGridSpec(
            num_scalar_prefetch=2,
            grid=(slots // block,),
            in_specs=[volume_spec, tile_spec],
            out_specs=pl.BlockSpec((slots + 2, rows, slices), lambda s, *_: (0, 0, 0)),
            scratch_shapes=[pltpu.VMEM((slots, rows, slices), jnp.float32)],
        ),
    )(first, pixel, volume, projector)
    f32, bf16 = jnp.float32, jnp.bfloat16
    dma = pltpu.SemaphoreType.DMA
    vmem = pl.BlockSpec(memory_space=pltpu.VMEM)
    smem = pl.BlockSpec(memory_space=pltpu.SMEM)
    scratch = (
        [pltpu.VMEM((slots + 2, depth, slices), jnp.int16)] * pieces
        + [pltpu.VMEM((pieces, n, band + 1, depth, slices), jnp.int16)] * 3
        + [pltpu.VMEM((pieces, rays, depth, slices), f32)]
        + [pltpu.VMEM((rays, depth, slices), bf16)] * pieces
        + [pltpu.VMEM((slots, depth, slices), bf16)] * (2 * pieces)
        + [pltpu.VMEM((owned, rows // 2, slices), bf16), pltpu.VMEM((rows // 2, 128), f32)]
        + [dma((pieces,)), dma((pieces,)), dma((2,)), dma((2,))]
        + [dma((pieces, n))] * 6
        + [dma((pieces,)), dma((pieces,))]
    )
    slot_residual = pl.pallas_call(
        functools.partial(exchange_kernel, n, pieces),
        out_shape=jax.ShapeDtypeStruct((slots, rows, slices), bf16),
        in_specs=[smem, smem, vmem, vmem, vmem],
        out_specs=vmem,
        scratch_shapes=scratch,
        compiler_params=pltpu.CompilerParams(collective_id=0, has_side_effects=True),
    )(own_idx, mate_idx, packed, sinogram, weights)
    return pl.pallas_call(
        backward_kernel,
        out_shape=jax.ShapeDtypeStruct(volume.shape, f32),
        grid_spec=pltpu.PrefetchScalarGridSpec(
            num_scalar_prefetch=1,
            grid=(slots // block,),
            in_specs=[
                volume_spec,
                tile_spec,
                pl.BlockSpec((block, rows, slices), lambda s, *_: (s, 0, 0)),
            ],
            out_specs=pl.BlockSpec(volume.shape, lambda s, *_: (0, 0, 0)),
            scratch_shapes=[pltpu.VMEM((patch_tiles, cols, 2 * slices), f32)],
        ),
    )(pixel, volume, projector, slot_residual)


def on_device(volume, projector, slot_ray, slot_pixel, sinogram, weight_index, weight_table):
    inners = lax.axis_size("inner")
    outers = lax.axis_size("outer")
    capacity = 2 * projector.shape[0] // inners
    dense = sinogram.shape[0] * outers <= capacity
    path = paired_path if outers == 2 and dense else general_path
    return path(volume, projector, slot_ray, slot_pixel, sinogram, weight_index, weight_table)


def solution(mesh):
    in_specs = (
        P(("group", "inner", "outer"), None, "cuts"),
        P(("inner", "outer"), None, None, None),
        P(("inner", "outer")),
        P(("inner", "outer"), None),
        P(("group", "inner", "outer"), None, "cuts"),
        P(("group", "inner", "outer"), None),
        P(),
    )
    out_specs = P(("group", "inner", "outer"), None, "cuts")
    return jax.shard_map(
        on_device, mesh=mesh, in_specs=in_specs, out_specs=out_specs, check_vma=False
    )
```

```python
import functools

import jax
import jax.numpy as jnp
from jax import lax
from jax.experimental import pallas as pl
from jax.experimental.pallas import tpu as pltpu
from jax.sharding import PartitionSpec as P

MESH = pl.DeviceIdType.MESH
PIECE = 16
LIMIT = 32000.0


def general_path(volume, projector, slot_ray, slot_pixel, sinogram, weight_index, weight_table):
    inners = lax.axis_size("inner")
    outers = lax.axis_size("outer")
    slot_count = projector.shape[0]
    per_slot = projector.shape[1]
    tile_rows = projector.shape[2]
    tile_cols = projector.shape[3]
    patch_tiles = volume.shape[0]
    slice_count = volume.shape[2]
    owned_rows = sinogram.shape[0]
    band_rows = owned_rows * outers
    capacity = 2 * slot_count // inners
    cell_count = inners * capacity
    target = slot_ray // band_rows
    offset = slot_ray % band_rows
    same_target = target[:, None] == target[None, :]
    earlier = jnp.arange(slot_count)[:, None] > jnp.arange(slot_count)[None, :]
    slot_rank = jnp.sum(jnp.logical_and(same_target, earlier), axis=1)
    position = target * capacity + slot_rank
    partial_value = jnp.zeros((slot_count, tile_rows, slice_count), jnp.float32)
    for column in range(per_slot):
        pixels = volume[slot_pixel[:, column]]
        partial_value = partial_value + jnp.einsum(
            "srp,spc->src", projector[:, column], pixels, preferred_element_type=jnp.float32
        )
    outgoing = (
        jnp.zeros((cell_count, tile_rows, slice_count), jnp.float32).at[position].set(partial_value)
    )
    labels = jnp.full((cell_count,), -1.0, jnp.float32).at[position].set(offset.astype(jnp.float32))
    arrived, arrived_rows = (
        lax.all_to_all(
            outgoing.reshape(inners, capacity, tile_rows, slice_count),
            "inner",
            split_axis=0,
            concat_axis=0,
            tiled=True,
        ),
        lax.all_to_all(
            labels.reshape(inners, capacity), "inner", split_axis=0, concat_axis=0, tiled=True
        ),
    )
    selector = (
        jnp.arange(band_rows, dtype=jnp.float32)[:, None] == arrived_rows.reshape(1, cell_count)
    ).astype(jnp.float32)
    block_sums = jnp.dot(
        selector,
        arrived.reshape(cell_count, tile_rows * slice_count),
        precision=lax.Precision.HIGHEST,
    ).reshape(band_rows, tile_rows, slice_count)
    classes = weight_table.shape[0]
    lookup = weight_index[:, :, None] == jnp.arange(classes)[None, None, :]
    weights = jnp.sum(
        jnp.where(lookup, weight_table[None, None, :], jnp.zeros((), weight_table.dtype)), axis=2
    )
    own_sums = lax.psum_scatter(block_sums, "outer", scatter_dimension=0, tiled=True)
    own_residual = (
        weights.astype(jnp.float32)[:, :, None] * (sinogram.astype(jnp.float32) - own_sums)
    ).astype(jnp.bfloat16)
    residual = lax.all_gather(own_residual, "outer", axis=0, tiled=True)
    picked = jnp.dot(
        selector.T.astype(jnp.bfloat16),
        residual.reshape(band_rows, tile_rows * slice_count),
        preferred_element_type=jnp.float32,
    ).astype(jnp.bfloat16)
    returned = lax.all_to_all(
        picked.reshape(inners, capacity, tile_rows, slice_count),
        "inner",
        split_axis=0,
        concat_axis=0,
        tiled=True,
    )
    slot_residual = returned.reshape(cell_count, tile_rows, slice_count)[position]
    owners = jnp.arange(patch_tiles)
    backward = jnp.zeros((patch_tiles, tile_cols, slice_count), jnp.float32)
    column_sum = jnp.zeros((patch_tiles, tile_cols), jnp.float32)
    for column in range(per_slot):
        member = (owners[:, None] == slot_pixel[None, :, column]).astype(jnp.float32)
        spread = jnp.einsum(
            "srp,src->spc", projector[:, column], slot_residual, preferred_element_type=jnp.float32
        )
        backward = backward + jnp.einsum(
            "ts,spc->tpc", member, spread, precision=lax.Precision.HIGHEST
        )
        column_sum = column_sum + jnp.dot(
            member,
            jnp.sum(projector[:, column], axis=1, dtype=jnp.float32),
            precision=lax.Precision.HIGHEST,
        )
    return volume.astype(jnp.float32) + backward / column_sum[:, :, None]


def exponent_of(largest):
    top = jnp.max(largest, axis=0, keepdims=True)
    exponent = jnp.ceil(jnp.log2(jnp.maximum(top, 1e-20) * (1.0 / LIMIT)))
    return jnp.broadcast_to(exponent, largest.shape)


def encode(value, inverse):
    return jnp.round(value * inverse).astype(jnp.int32).astype(jnp.int16)


def decode(coded):
    return coded.astype(jnp.int32).astype(jnp.float32)


def forward_kernel(
    ray_ref, pixel_ref, table_ref, index_ref, volume_ref, projector_ref, coded_ref, own_ref, wts_ref,
    packed_ref,
):
    step = pl.program_id(0)
    block, per_slot = projector_ref.shape[:2]
    slots, rows, slices = packed_ref.shape
    rays = own_ref.shape[0] - slots

    @pl.when(step == 0)
    def _():
        packed_ref[...] = jnp.zeros_like(packed_ref)

        def clear(r, carry):
            own_ref[slots + r] = slots
            return carry

        lax.fori_loop(0, rays, clear, 0, unroll=8)

        def enter(k, carry):
            s = slots - 1 - k
            own_ref[s] = ray_ref[s]
            own_ref[slots + ray_ref[s]] = s
            return carry

        lax.fori_loop(0, slots, enter, 0, unroll=4)
        index = index_ref[...]
        weight = jnp.zeros(index.shape, jnp.float32)
        for k in range(table_ref.shape[0]):
            weight = jnp.where(index == k, table_ref[k], weight)
        blank = jnp.zeros((rows - index.shape[0], rows), jnp.float32)
        wts_ref[...] = jnp.concatenate([weight, blank], axis=0).T

    for j in range(block):
        s = step * block + j
        pixels = jnp.concatenate(
            [volume_ref[pixel_ref[g, s]] for g in range(per_slot)], axis=0
        )
        tiles = jnp.concatenate([projector_ref[j, g] for g in range(per_slot)], axis=1)
        cell = own_ref[slots + ray_ref[s]]
        packed_ref[cell] += jnp.dot(tiles, pixels, preferred_element_type=jnp.float32)

    @pl.when(step == pl.num_programs(0) - 1)
    def _():
        largest = jnp.zeros((PIECE, slices), jnp.float32)
        for s in range(slots):
            for r in range(0, rows, PIECE):
                largest = jnp.maximum(largest, jnp.abs(packed_ref[s, r : r + PIECE]))
        exponent = exponent_of(largest)
        inverse = jnp.exp2(-exponent)
        for s in range(slots):
            for r in range(0, rows, PIECE):
                coded_ref[s, r : r + PIECE] = encode(packed_ref[s, r : r + PIECE], inverse)
        for r in range(0, rows, PIECE):
            coded_ref[slots, r : r + PIECE] = jnp.zeros((PIECE, slices), jnp.int16)
            coded_ref[slots + 1, r : r + PIECE] = exponent.astype(jnp.int32).astype(jnp.int16)


def backward_kernel(pixel_ref, volume_ref, projector_ref, residual_ref, out_ref, acc_ref):
    step = pl.program_id(0)
    block, per_slot, rows, cols = projector_ref.shape
    slices = residual_ref.shape[-1]

    @pl.when(step == 0)
    def _():
        acc_ref[...] = jnp.zeros_like(acc_ref)

    ones = jnp.ones((PIECE, rows), jnp.bfloat16)
    for j in range(block):
        s = step * block + j
        tall = jnp.concatenate([residual_ref[j].T, ones], axis=0)
        tiles = jnp.concatenate([projector_ref[j, g] for g in range(per_slot)], axis=1)
        spread = jnp.dot(tall, tiles, preferred_element_type=jnp.float32)
        for g in range(per_slot):
            acc_ref[pixel_ref[g, s]] += spread[:, g * cols : (g + 1) * cols]

    @pl.when(step == pl.num_programs(0) - 1)
    def _():
        for q in range(acc_ref.shape[0]):
            update = acc_ref[q, :slices] / acc_ref[q, slices : slices + 1]
            out_ref[q] = volume_ref[q].astype(jnp.float32) + update.T


def exchange_kernel(n, pieces, own_idx, packed, sino, wts, out_ref, *scratch):
    take = iter(scratch)
    mate_part = [next(take) for _ in range(pieces)]
    from_left, from_right, going, dense = (next(take) for _ in range(4))
    band_res = [next(take) for _ in range(pieces)]
    picked = [next(take) for _ in range(pieces)]
    landed = [next(take) for _ in range(pieces)]
    mate_sino, mate_wts, mate_idx = (next(take) for _ in range(3))
    x_send, x_recv, aux_send, aux_recv, sum_send, left_recv, right_recv = (
        next(take) for _ in range(7)
    )
    out_right, out_left, res_recv, pick_send, pick_recv = (next(take) for _ in range(5))

    slots, rows, slices = out_ref.shape
    owned = sino.shape[0]
    band = 2 * owned
    half = rows // 2
    depth = half // pieces
    i = lax.axis_index("inner")
    o = lax.axis_index("outer")
    mate = {"outer": 1 - o}
    right = {"inner": i + 1}
    left = {"inner": i - 1}

    def send(src, dst, ssem, rsem, device):
        return pltpu.make_async_remote_copy(
            src_ref=src, dst_ref=dst, send_sem=ssem, recv_sem=rsem, device_id=device,
            device_id_type=MESH,
        )

    barrier = pltpu.get_barrier_semaphore()
    pl.semaphore_signal(barrier, inc=1, device_id=mate, device_id_type=MESH)

    @pl.when(i > 0)
    def _():
        pl.semaphore_signal(barrier, inc=1, device_id=left, device_id_type=MESH)

    @pl.when(i < n - 1)
    def _():
        pl.semaphore_signal(barrier, inc=1, device_id=right, device_id_type=MESH)

    pl.semaphore_wait(barrier, jnp.where(i > 0, 2, 1) + jnp.where(i < n - 1, 1, 0))

    def mine(c):
        return pl.ds(pl.multiple_of(o * half + c * depth, depth), depth)

    def theirs(c):
        return pl.ds(pl.multiple_of((1 - o) * half + c * depth, depth), depth)

    def swap(c):
        return send(
            packed.at[:, theirs(c)],
            mate_part[c],
            x_send.at[c],
            x_recv.at[c],
            mate,
        )

    other_half = pl.ds(pl.multiple_of((1 - o) * half, half), half)
    aux = [
        send(sino.at[:, other_half], mate_sino, aux_send.at[0], aux_recv.at[0], mate),
        send(wts.at[other_half], mate_wts, aux_send.at[1], aux_recv.at[1], mate),
    ]
    table = send(own_idx, mate_idx, aux_send.at[2], aux_recv.at[2], mate)
    table.start()
    for c in range(pieces):
        swap(c).start()
        if c == min(1, pieces - 1):
            for copy in aux:
                copy.start()
    def local_scales(c):
        return (
            jnp.exp2(decode(packed[slots + 1, mine(c), :])),
            jnp.exp2(decode(mate_part[c][slots + 1])),
        )

    def local(c, r, scales):
        return (
            decode(packed[own_idx[slots + r], mine(c), :]) * scales[0]
            + decode(mate_part[c][mate_idx[slots + r]]) * scales[1]
        )

    def loop(count, body):
        def step(t, carry):
            body(t)
            return carry

        lax.fori_loop(0, count, step, 0, unroll=4)

    def go_right(c, b):
        return send(
            going.at[c, b], from_left.at[c, b], sum_send.at[c, b], left_recv.at[c, b], right
        )

    def go_left(c, b):
        return send(
            going.at[c, b], from_right.at[c, b], sum_send.at[c, b], right_recv.at[c, b], left
        )

    def gather(c):
        swap(c).wait_recv()
        scales = local_scales(c)

        def fill(r):
            dense[c, r] = local(c, r, scales)

        loop(n * band, fill)

    def hop(c, b, to_right):
        copy = (go_right if to_right else go_left)(c, b)
        arrived = from_left if to_right else from_right

        def widest(t, largest):
            return jnp.maximum(largest, jnp.abs(dense[c, b * band + t]))

        @pl.when(i > 0 if to_right else i < n - 1)
        def _():
            copy.wait_recv()
            scale = jnp.exp2(decode(arrived[c, b, band]))

            def add(t):
                dense[c, b * band + t] += decode(arrived[c, b, t]) * scale

            loop(band, add)

        exponent = exponent_of(
            lax.fori_loop(0, band, widest, jnp.zeros((depth, slices), jnp.float32), unroll=4)
        )
        inverse = jnp.exp2(-exponent)

        def pack(t):
            going[c, b, t] = encode(dense[c, b * band + t], inverse)

        loop(band, pack)
        going[c, b, band] = exponent.astype(jnp.int32).astype(jnp.int16)
        copy.start()

    def sums(step):
        def rightward(far, carry):
            hop(step - i, n - 1 - far, True)
            return carry

        def leftward(far, carry):
            hop(step - (n - 1 - i), far, False)
            return carry

        @pl.when(jnp.logical_and(step >= i, step - i < pieces))
        def _():
            lax.fori_loop(0, n - 1 - i, rightward, 0)

        @pl.when(jnp.logical_and(step >= n - 1 - i, step - (n - 1 - i) < pieces))
        def _():
            lax.fori_loop(0, i, leftward, 0)

    def share_right(c, b):
        part = band_res[c].at[pl.ds(pl.multiple_of(b * band, band), band)]
        return send(part, part, out_right.at[c, b], res_recv.at[c, b], right)

    def share_left(c, b):
        part = band_res[c].at[pl.ds(pl.multiple_of(b * band, band), band)]
        return send(part, part, out_left.at[c, b], res_recv.at[c, b], left)

    def finish(c):
        @pl.when(i > 0)
        def _():
            go_right(c, i).wait_recv()

            scale = jnp.exp2(decode(from_left[c, i, band]))

            def add(t):
                dense[c, i * band + t] += decode(from_left[c, i, t]) * scale

            loop(band, add)

        @pl.when(i < n - 1)
        def _():
            go_left(c, i).wait_recv()

            scale = jnp.exp2(decode(from_right[c, i, band]))

            def add(t):
                dense[c, i * band + t] += decode(from_right[c, i, t]) * scale

            loop(band, add)

        if c == 0:
            for copy in aux:
                copy.wait_recv()
        for j in range(owned):
            t = o * owned + j
            weight = wts[mine(c), j : j + 1]
            value = weight * (sino[j, mine(c), :].astype(jnp.float32) - dense[c, i * band + t])
            band_res[c][i * band + t] = value.astype(jnp.bfloat16)
            t = (1 - o) * owned + j
            rows_here = pl.ds(c * depth, depth)
            weight = mate_wts[rows_here, j : j + 1]
            value = weight * (mate_sino[j, rows_here, :].astype(jnp.float32) - dense[c, i * band + t])
            band_res[c][i * band + t] = value.astype(jnp.bfloat16)

        @pl.when(i < n - 1)
        def _():
            share_right(c, i).start()

        @pl.when(i > 0)
        def _():
            share_left(c, i).start()

    def relay(c, d):
        @pl.when(i - d >= 0)
        def _():
            share_right(c, i - d).wait_recv()

            @pl.when(i < n - 1)
            def _():
                share_right(c, i - d).start()

        @pl.when(i + d <= n - 1)
        def _():
            share_left(c, i + d).wait_recv()

            @pl.when(i > 0)
            def _():
                share_left(c, i + d).start()

    def give(c):
        return send(picked[c], landed[c], pick_send.at[c], pick_recv.at[c], mate)

    def pick(c):
        def for_mate(k):
            picked[c][k] = band_res[c][mate_idx[k]]

        loop(slots, for_mate)
        give(c).start()

        def for_self(k):
            out_ref[k, mine(c), :] = band_res[c][own_idx[k]]

        loop(slots, for_self)

    def collect(c):
        give(c).wait_recv()

        def copy_in(k):
            out_ref[k, theirs(c), :] = landed[c][k]

        loop(slots, copy_in)

    table.wait_recv()
    for step in range(pieces + 2 * (n - 1)):
        if step < pieces:
            gather(step)
        if step < pieces + n - 1:
            sums(step)
        for d in range(n):
            c = step - (n - 1) - d
            if 0 <= c < pieces:
                if d == 0:
                    finish(c)
                else:
                    relay(c, d)
                if d == n - 1:
                    pick(c)
    for c in range(pieces):
        collect(c)

    for copy in aux + [table]:
        copy.wait_send()
    for c in range(pieces):
        swap(c).wait_send()
        give(c).wait_send()
        for b in range(n):

            @pl.when(b > i)
            def _():
                go_right(c, b).wait_send()

            @pl.when(b < i)
            def _():
                go_left(c, b).wait_send()

            @pl.when(jnp.logical_and(b <= i, i < n - 1))
            def _():
                share_right(c, b).wait_send()

            @pl.when(jnp.logical_and(b >= i, i > 0))
            def _():
                share_left(c, b).wait_send()


def paired_path(volume, projector, slot_ray, slot_pixel, sinogram, weight_index, weight_table):
    n = lax.axis_size("inner")
    slots, per_slot, rows, cols = projector.shape
    patch_tiles, _, slices = volume.shape
    owned = sinogram.shape[0]
    band = 2 * owned
    rays = n * band
    pieces = rows // 2 // PIECE
    depth = PIECE
    pixel = slot_pixel.T
    block = 8
    tile_spec = pl.BlockSpec((block, per_slot, rows, cols), lambda s, *_: (s, 0, 0, 0))
    volume_spec = pl.BlockSpec(volume.shape, lambda s, *_: (0, 0, 0))
    whole = lambda shape: pl.BlockSpec(shape, lambda s, *_: (0,) * len(shape))
    coded_shape = (slots + 2, rows, slices)
    packed, own_idx, weights = pl.pallas_call(
        forward_kernel,
        out_shape=(
            jax.ShapeDtypeStruct(coded_shape, jnp.int16),
            jax.ShapeDtypeStruct((slots + rays,), jnp.int32),
            jax.ShapeDtypeStruct((rows, rows), jnp.float32),
        ),
        grid_spec=pltpu.PrefetchScalarGridSpec(
            num_scalar_prefetch=3,
            grid=(slots // block,),
            in_specs=[whole(weight_index.shape), volume_spec, tile_spec],
            out_specs=(
                whole(coded_shape),
                pl.BlockSpec(memory_space=pltpu.SMEM),
                whole((rows, rows)),
            ),
            scratch_shapes=[pltpu.VMEM((slots, rows, slices), jnp.float32)],
        ),
    )(slot_ray, pixel, weight_table.astype(jnp.float32), weight_index, volume, projector)
    f32, bf16 = jnp.float32, jnp.bfloat16
    dma = pltpu.SemaphoreType.DMA
    vmem = pl.BlockSpec(memory_space=pltpu.VMEM)
    smem = pl.BlockSpec(memory_space=pltpu.SMEM)
    scratch = (
        [pltpu.VMEM((slots + 2, depth, slices), jnp.int16)] * pieces
        + [pltpu.VMEM((pieces, n, band + 1, depth, slices), jnp.int16)] * 3
        + [pltpu.VMEM((pieces, rays, depth, slices), f32)]
        + [pltpu.VMEM((rays, depth, slices), bf16)] * pieces
        + [pltpu.VMEM((slots, depth, slices), bf16)] * (2 * pieces)
        + [pltpu.VMEM((owned, rows // 2, slices), bf16), pltpu.VMEM((rows // 2, 128), f32)]
        + [pltpu.SMEM((slots + rays,), jnp.int32)]
        + [dma((pieces,)), dma((pieces,)), dma((3,)), dma((3,))]
        + [dma((pieces, n))] * 6
        + [dma((pieces,)), dma((pieces,))]
    )
    slot_residual = pl.pallas_call(
        functools.partial(exchange_kernel, n, pieces),
        out_shape=jax.ShapeDtypeStruct((slots, rows, slices), bf16),
        in_specs=[smem, vmem, vmem, vmem],
        out_specs=vmem,
        scratch_shapes=scratch,
        compiler_params=pltpu.CompilerParams(collective_id=0, has_side_effects=True),
    )(own_idx, packed, sinogram, weights)
    return pl.pallas_call(
        backward_kernel,
        out_shape=jax.ShapeDtypeStruct(volume.shape, f32),
        grid_spec=pltpu.PrefetchScalarGridSpec(
            num_scalar_prefetch=1,
            grid=(slots // block,),
            in_specs=[
                volume_spec,
                tile_spec,
                pl.BlockSpec((block, rows, slices), lambda s, *_: (s, 0, 0)),
            ],
            out_specs=pl.BlockSpec(volume.shape, lambda s, *_: (0, 0, 0)),
            scratch_shapes=[pltpu.VMEM((patch_tiles, slices + PIECE, cols), f32)],
        ),
    )(pixel, volume, projector, slot_residual)


def on_device(volume, projector, slot_ray, slot_pixel, sinogram, weight_index, weight_table):
    inners = lax.axis_size("inner")
    outers = lax.axis_size("outer")
    capacity = 2 * projector.shape[0] // inners
    dense = sinogram.shape[0] * outers <= capacity
    path = paired_path if outers == 2 and dense else general_path
    return path(volume, projector, slot_ray, slot_pixel, sinogram, weight_index, weight_table)


def solution(mesh):
    in_specs = (
        P(("group", "inner", "outer"), None, "cuts"),
        P(("inner", "outer"), None, None, None),
        P(("inner", "outer")),
        P(("inner", "outer"), None),
        P(("group", "inner", "outer"), None, "cuts"),
        P(("group", "inner", "outer"), None),
        P(),
    )
    out_specs = P(("group", "inner", "outer"), None, "cuts")
    return jax.shard_map(
        on_device, mesh=mesh, in_specs=in_specs, out_specs=out_specs, check_vma=False
    )
```

```python
import functools

import jax
import jax.numpy as jnp
from jax import lax
from jax.experimental import pallas as pl
from jax.experimental.pallas import tpu as pltpu
from jax.sharding import PartitionSpec as P

MESH = pl.DeviceIdType.MESH
PIECE = 16
LIMIT = 32000.0


def general_path(volume, projector, slot_ray, slot_pixel, sinogram, weight_index, weight_table):
    inners = lax.axis_size("inner")
    outers = lax.axis_size("outer")
    slot_count = projector.shape[0]
    per_slot = projector.shape[1]
    tile_rows = projector.shape[2]
    tile_cols = projector.shape[3]
    patch_tiles = volume.shape[0]
    slice_count = volume.shape[2]
    owned_rows = sinogram.shape[0]
    band_rows = owned_rows * outers
    capacity = 2 * slot_count // inners
    cell_count = inners * capacity
    target = slot_ray // band_rows
    offset = slot_ray % band_rows
    same_target = target[:, None] == target[None, :]
    earlier = jnp.arange(slot_count)[:, None] > jnp.arange(slot_count)[None, :]
    slot_rank = jnp.sum(jnp.logical_and(same_target, earlier), axis=1)
    position = target * capacity + slot_rank
    partial_value = jnp.zeros((slot_count, tile_rows, slice_count), jnp.float32)
    for column in range(per_slot):
        pixels = volume[slot_pixel[:, column]]
        partial_value = partial_value + jnp.einsum(
            "srp,spc->src", projector[:, column], pixels, preferred_element_type=jnp.float32
        )
    outgoing = (
        jnp.zeros((cell_count, tile_rows, slice_count), jnp.float32).at[position].set(partial_value)
    )
    labels = jnp.full((cell_count,), -1.0, jnp.float32).at[position].set(offset.astype(jnp.float32))
    arrived, arrived_rows = (
        lax.all_to_all(
            outgoing.reshape(inners, capacity, tile_rows, slice_count),
            "inner",
            split_axis=0,
            concat_axis=0,
            tiled=True,
        ),
        lax.all_to_all(
            labels.reshape(inners, capacity), "inner", split_axis=0, concat_axis=0, tiled=True
        ),
    )
    selector = (
        jnp.arange(band_rows, dtype=jnp.float32)[:, None] == arrived_rows.reshape(1, cell_count)
    ).astype(jnp.float32)
    block_sums = jnp.dot(
        selector,
        arrived.reshape(cell_count, tile_rows * slice_count),
        precision=lax.Precision.HIGHEST,
    ).reshape(band_rows, tile_rows, slice_count)
    classes = weight_table.shape[0]
    lookup = weight_index[:, :, None] == jnp.arange(classes)[None, None, :]
    weights = jnp.sum(
        jnp.where(lookup, weight_table[None, None, :], jnp.zeros((), weight_table.dtype)), axis=2
    )
    own_sums = lax.psum_scatter(block_sums, "outer", scatter_dimension=0, tiled=True)
    own_residual = (
        weights.astype(jnp.float32)[:, :, None] * (sinogram.astype(jnp.float32) - own_sums)
    ).astype(jnp.bfloat16)
    residual = lax.all_gather(own_residual, "outer", axis=0, tiled=True)
    picked = jnp.dot(
        selector.T.astype(jnp.bfloat16),
        residual.reshape(band_rows, tile_rows * slice_count),
        preferred_element_type=jnp.float32,
    ).astype(jnp.bfloat16)
    returned = lax.all_to_all(
        picked.reshape(inners, capacity, tile_rows, slice_count),
        "inner",
        split_axis=0,
        concat_axis=0,
        tiled=True,
    )
    slot_residual = returned.reshape(cell_count, tile_rows, slice_count)[position]
    owners = jnp.arange(patch_tiles)
    backward = jnp.zeros((patch_tiles, tile_cols, slice_count), jnp.float32)
    column_sum = jnp.zeros((patch_tiles, tile_cols), jnp.float32)
    for column in range(per_slot):
        member = (owners[:, None] == slot_pixel[None, :, column]).astype(jnp.float32)
        spread = jnp.einsum(
            "srp,src->spc", projector[:, column], slot_residual, preferred_element_type=jnp.float32
        )
        backward = backward + jnp.einsum(
            "ts,spc->tpc", member, spread, precision=lax.Precision.HIGHEST
        )
        column_sum = column_sum + jnp.dot(
            member,
            jnp.sum(projector[:, column], axis=1, dtype=jnp.float32),
            precision=lax.Precision.HIGHEST,
        )
    return volume.astype(jnp.float32) + backward / column_sum[:, :, None]


def exponent_of(largest):
    top = jnp.max(largest, axis=0, keepdims=True)
    exponent = jnp.ceil(jnp.log2(jnp.maximum(top, 1e-20) * (1.0 / LIMIT)))
    return jnp.broadcast_to(exponent, largest.shape)


def encode(value, inverse):
    return jnp.round(value * inverse).astype(jnp.int32).astype(jnp.int16)


def decode(coded):
    return coded.astype(jnp.int32).astype(jnp.float32)


def forward_kernel(
    ray_ref, pixel_ref, index_ref, table_ref, volume_ref, projector_ref, coded_ref, own_ref, wts_ref,
    packed_ref,
):
    step = pl.program_id(0)
    block, per_slot = projector_ref.shape[:2]
    slots, rows, slices = packed_ref.shape
    rays = own_ref.shape[0] - slots

    @pl.when(step == 0)
    def _():
        packed_ref[...] = jnp.zeros_like(packed_ref)

        def clear(r, carry):
            own_ref[slots + r] = slots
            return carry

        lax.fori_loop(0, rays, clear, 0, unroll=8)

        def enter(k, carry):
            s = slots - 1 - k
            own_ref[s] = ray_ref[s]
            own_ref[slots + ray_ref[s]] = s
            return carry

        lax.fori_loop(0, slots, enter, 0, unroll=4)
        index = index_ref[...]
        weight = jnp.zeros(index.shape, jnp.float32)
        table = table_ref[...].astype(jnp.float32)
        for k in range(table.shape[1]):
            weight = jnp.where(index == k, table[:, k : k + 1], weight)
        blank = jnp.zeros((rows - index.shape[0], rows), jnp.float32)
        wts_ref[...] = jnp.concatenate([weight, blank], axis=0).T

    for j in range(block):
        s = step * block + j
        pixels = jnp.concatenate(
            [volume_ref[pixel_ref[g, s]] for g in range(per_slot)], axis=0
        )
        tiles = jnp.concatenate([projector_ref[j, g] for g in range(per_slot)], axis=1)
        cell = own_ref[slots + ray_ref[s]]
        packed_ref[cell] += jnp.dot(tiles, pixels, preferred_element_type=jnp.float32)

    @pl.when(step == pl.num_programs(0) - 1)
    def _():
        largest = jnp.zeros((PIECE, slices), jnp.float32)
        for s in range(slots):
            for r in range(0, rows, PIECE):
                largest = jnp.maximum(largest, jnp.abs(packed_ref[s, r : r + PIECE]))
        exponent = exponent_of(largest)
        inverse = jnp.exp2(-exponent)
        for s in range(slots):
            for r in range(0, rows, PIECE):
                coded_ref[s, r : r + PIECE] = encode(packed_ref[s, r : r + PIECE], inverse)
        for r in range(0, rows, PIECE):
            coded_ref[slots, r : r + PIECE] = jnp.zeros((PIECE, slices), jnp.int16)
            coded_ref[slots + 1, r : r + PIECE] = exponent.astype(jnp.int32).astype(jnp.int16)


def backward_kernel(pixel_ref, volume_ref, projector_ref, residual_ref, out_ref, acc_ref):
    step = pl.program_id(0)
    block, per_slot, rows, cols = projector_ref.shape
    slices = residual_ref.shape[-1]

    @pl.when(step == 0)
    def _():
        acc_ref[...] = jnp.zeros_like(acc_ref)

    ones = jnp.ones((PIECE, rows), jnp.bfloat16)
    for j in range(block):
        s = step * block + j
        tall = jnp.concatenate([residual_ref[j].T, ones], axis=0)
        tiles = jnp.concatenate([projector_ref[j, g] for g in range(per_slot)], axis=1)
        spread = jnp.dot(tall, tiles, preferred_element_type=jnp.float32)
        for g in range(per_slot):
            acc_ref[pixel_ref[g, s]] += spread[:, g * cols : (g + 1) * cols]

    @pl.when(step == pl.num_programs(0) - 1)
    def _():
        for q in range(acc_ref.shape[0]):
            update = acc_ref[q, :slices] / acc_ref[q, slices : slices + 1]
            out_ref[q] = volume_ref[q].astype(jnp.float32) + update.T


def exchange_kernel(n, pieces, own_idx, packed, sino, wts, out_ref, *scratch):
    take = iter(scratch)
    mate_part = [next(take) for _ in range(pieces)]
    from_left, from_right, going, dense = (next(take) for _ in range(4))
    band_res = [next(take) for _ in range(pieces)]
    picked = [next(take) for _ in range(pieces)]
    landed = [next(take) for _ in range(pieces)]
    mate_sino, mate_wts, mate_idx = (next(take) for _ in range(3))
    x_send, x_recv, aux_send, aux_recv, sum_send, left_recv, right_recv = (
        next(take) for _ in range(7)
    )
    out_right, out_left, res_recv, pick_send, pick_recv = (next(take) for _ in range(5))

    slots, rows, slices = out_ref.shape
    owned = sino.shape[0]
    band = 2 * owned
    half = rows // 2
    depth = half // pieces
    i = lax.axis_index("inner")
    o = lax.axis_index("outer")
    mate = {"outer": 1 - o}
    right = {"inner": i + 1}
    left = {"inner": i - 1}

    def send(src, dst, ssem, rsem, device):
        return pltpu.make_async_remote_copy(
            src_ref=src, dst_ref=dst, send_sem=ssem, recv_sem=rsem, device_id=device,
            device_id_type=MESH,
        )

    barrier = pltpu.get_barrier_semaphore()
    pl.semaphore_signal(barrier, inc=1, device_id=mate, device_id_type=MESH)

    @pl.when(i > 0)
    def _():
        pl.semaphore_signal(barrier, inc=1, device_id=left, device_id_type=MESH)

    @pl.when(i < n - 1)
    def _():
        pl.semaphore_signal(barrier, inc=1, device_id=right, device_id_type=MESH)

    pl.semaphore_wait(barrier, jnp.where(i > 0, 2, 1) + jnp.where(i < n - 1, 1, 0))

    def mine(c):
        return pl.ds(pl.multiple_of(o * half + c * depth, depth), depth)

    def theirs(c):
        return pl.ds(pl.multiple_of((1 - o) * half + c * depth, depth), depth)

    def swap(c):
        return send(
            packed.at[:, theirs(c)],
            mate_part[c],
            x_send.at[c],
            x_recv.at[c],
            mate,
        )

    other_half = pl.ds(pl.multiple_of((1 - o) * half, half), half)
    aux = [
        send(sino.at[:, other_half], mate_sino, aux_send.at[0], aux_recv.at[0], mate),
        send(wts.at[other_half], mate_wts, aux_send.at[1], aux_recv.at[1], mate),
    ]
    table = send(own_idx, mate_idx, aux_send.at[2], aux_recv.at[2], mate)
    table.start()
    for c in range(pieces):
        swap(c).start()
        if c == min(1, pieces - 1):
            for copy in aux:
                copy.start()
    def local_scales(c):
        return (
            jnp.exp2(decode(packed[slots + 1, mine(c), :])),
            jnp.exp2(decode(mate_part[c][slots + 1])),
        )

    def local(c, r, scales):
        return (
            decode(packed[own_idx[slots + r], mine(c), :]) * scales[0]
            + decode(mate_part[c][mate_idx[slots + r]]) * scales[1]
        )

    def loop(count, body):
        def step(t, carry):
            body(t)
            return carry

        lax.fori_loop(0, count, step, 0, unroll=4)

    def go_right(c, b):
        return send(
            going.at[c, b], from_left.at[c, b], sum_send.at[c, b], left_recv.at[c, b], right
        )

    def go_left(c, b):
        return send(
            going.at[c, b], from_right.at[c, b], sum_send.at[c, b], right_recv.at[c, b], left
        )

    def gather(c):
        swap(c).wait_recv()
        scales = local_scales(c)

        def fill(r):
            dense[c, r] = local(c, r, scales)

        loop(n * band, fill)

    def hop(c, b, to_right):
        copy = (go_right if to_right else go_left)(c, b)
        arrived = from_left if to_right else from_right

        def widest(t, largest):
            return jnp.maximum(largest, jnp.abs(dense[c, b * band + t]))

        @pl.when(i > 0 if to_right else i < n - 1)
        def _():
            copy.wait_recv()
            scale = jnp.exp2(decode(arrived[c, b, band]))

            def add(t):
                dense[c, b * band + t] += decode(arrived[c, b, t]) * scale

            loop(band, add)

        exponent = exponent_of(
            lax.fori_loop(0, band, widest, jnp.zeros((depth, slices), jnp.float32), unroll=4)
        )
        inverse = jnp.exp2(-exponent)

        def pack(t):
            going[c, b, t] = encode(dense[c, b * band + t], inverse)

        loop(band, pack)
        going[c, b, band] = exponent.astype(jnp.int32).astype(jnp.int16)
        copy.start()

    def sums(step):
        def rightward(far, carry):
            c = step - i - far
            pl.when(jnp.logical_and(c >= 0, c < pieces))(lambda: hop(c, n - 1 - far, True))
            return carry

        def leftward(far, carry):
            c = step - (n - 1 - i) - far
            pl.when(jnp.logical_and(c >= 0, c < pieces))(lambda: hop(c, far, False))
            return carry

        lax.fori_loop(0, n - 1 - i, rightward, 0)
        lax.fori_loop(0, i, leftward, 0)

    def share_right(c, b):
        part = band_res[c].at[pl.ds(pl.multiple_of(b * band, band), band)]
        return send(part, part, out_right.at[c, b], res_recv.at[c, b], right)

    def share_left(c, b):
        part = band_res[c].at[pl.ds(pl.multiple_of(b * band, band), band)]
        return send(part, part, out_left.at[c, b], res_recv.at[c, b], left)

    def finish(c):
        @pl.when(i > 0)
        def _():
            go_right(c, i).wait_recv()

            scale = jnp.exp2(decode(from_left[c, i, band]))

            def add(t):
                dense[c, i * band + t] += decode(from_left[c, i, t]) * scale

            loop(band, add)

        @pl.when(i < n - 1)
        def _():
            go_left(c, i).wait_recv()

            scale = jnp.exp2(decode(from_right[c, i, band]))

            def add(t):
                dense[c, i * band + t] += decode(from_right[c, i, t]) * scale

            loop(band, add)

        if c == 0:
            for copy in aux:
                copy.wait_recv()
        for j in range(owned):
            t = o * owned + j
            weight = wts[mine(c), j : j + 1]
            value = weight * (sino[j, mine(c), :].astype(jnp.float32) - dense[c, i * band + t])
            band_res[c][i * band + t] = value.astype(jnp.bfloat16)
            t = (1 - o) * owned + j
            rows_here = pl.ds(c * depth, depth)
            weight = mate_wts[rows_here, j : j + 1]
            value = weight * (mate_sino[j, rows_here, :].astype(jnp.float32) - dense[c, i * band + t])
            band_res[c][i * band + t] = value.astype(jnp.bfloat16)

        @pl.when(i < n - 1)
        def _():
            share_right(c, i).start()

        @pl.when(i > 0)
        def _():
            share_left(c, i).start()

    def relay(c, d):
        @pl.when(i - d >= 0)
        def _():
            share_right(c, i - d).wait_recv()

            @pl.when(i < n - 1)
            def _():
                share_right(c, i - d).start()

        @pl.when(i + d <= n - 1)
        def _():
            share_left(c, i + d).wait_recv()

            @pl.when(i > 0)
            def _():
                share_left(c, i + d).start()

    def give(c):
        return send(picked[c], landed[c], pick_send.at[c], pick_recv.at[c], mate)

    def pick(c):
        def for_mate(k):
            picked[c][k] = band_res[c][mate_idx[k]]

        loop(slots, for_mate)
        give(c).start()

        def for_self(k):
            out_ref[k, mine(c), :] = band_res[c][own_idx[k]]

        loop(slots, for_self)

    def collect(c):
        give(c).wait_recv()

        def copy_in(k):
            out_ref[k, theirs(c), :] = landed[c][k]

        loop(slots, copy_in)

    table.wait_recv()
    for step in range(pieces + 2 * (n - 1)):
        if step < pieces:
            gather(step)
        if step < pieces + n - 1:
            sums(step)
        for d in range(n):
            c = step - (n - 1) - d
            if 0 <= c < pieces:
                if d == 0:
                    finish(c)
                else:
                    relay(c, d)
                if d == n - 1:
                    pick(c)
    for c in range(pieces):
        collect(c)

    for copy in aux + [table]:
        copy.wait_send()
    for c in range(pieces):
        swap(c).wait_send()
        give(c).wait_send()
        for b in range(n):

            @pl.when(b > i)
            def _():
                go_right(c, b).wait_send()

            @pl.when(b < i)
            def _():
                go_left(c, b).wait_send()

            @pl.when(jnp.logical_and(b <= i, i < n - 1))
            def _():
                share_right(c, b).wait_send()

            @pl.when(jnp.logical_and(b >= i, i > 0))
            def _():
                share_left(c, b).wait_send()


def paired_path(volume, projector, slot_ray, slot_pixel, sinogram, weight_index, weight_table):
    n = lax.axis_size("inner")
    slots, per_slot, rows, cols = projector.shape
    patch_tiles, _, slices = volume.shape
    owned = sinogram.shape[0]
    band = 2 * owned
    rays = n * band
    pieces = rows // 2 // PIECE
    depth = PIECE
    pixel = slot_pixel.T
    classes = weight_table.shape[0]
    block = 8
    tile_spec = pl.BlockSpec((block, per_slot, rows, cols), lambda s, *_: (s, 0, 0, 0))
    volume_spec = pl.BlockSpec(volume.shape, lambda s, *_: (0, 0, 0))
    whole = lambda shape: pl.BlockSpec(shape, lambda s, *_: (0,) * len(shape))
    coded_shape = (slots + 2, rows, slices)
    packed, own_idx, weights = pl.pallas_call(
        forward_kernel,
        out_shape=(
            jax.ShapeDtypeStruct(coded_shape, jnp.int16),
            jax.ShapeDtypeStruct((slots + rays,), jnp.int32),
            jax.ShapeDtypeStruct((rows, rows), jnp.float32),
        ),
        grid_spec=pltpu.PrefetchScalarGridSpec(
            num_scalar_prefetch=2,
            grid=(slots // block,),
            in_specs=[whole(weight_index.shape), whole((1, classes)), volume_spec, tile_spec],
            out_specs=(
                whole(coded_shape),
                pl.BlockSpec(memory_space=pltpu.SMEM),
                whole((rows, rows)),
            ),
            scratch_shapes=[pltpu.VMEM((slots, rows, slices), jnp.float32)],
        ),
    )(slot_ray, pixel, weight_index, weight_table.reshape(1, classes), volume, projector)
    f32, bf16 = jnp.float32, jnp.bfloat16
    dma = pltpu.SemaphoreType.DMA
    vmem = pl.BlockSpec(memory_space=pltpu.VMEM)
    smem = pl.BlockSpec(memory_space=pltpu.SMEM)
    scratch = (
        [pltpu.VMEM((slots + 2, depth, slices), jnp.int16)] * pieces
        + [pltpu.VMEM((pieces, n, band + 1, depth, slices), jnp.int16)] * 3
        + [pltpu.VMEM((pieces, rays, depth, slices), f32)]
        + [pltpu.VMEM((rays, depth, slices), bf16)] * pieces
        + [pltpu.VMEM((slots, depth, slices), bf16)] * (2 * pieces)
        + [pltpu.VMEM((owned, rows // 2, slices), bf16), pltpu.VMEM((rows // 2, 128), f32)]
        + [pltpu.SMEM((slots + rays,), jnp.int32)]
        + [dma((pieces,)), dma((pieces,)), dma((3,)), dma((3,))]
        + [dma((pieces, n))] * 6
        + [dma((pieces,)), dma((pieces,))]
    )
    slot_residual = pl.pallas_call(
        functools.partial(exchange_kernel, n, pieces),
        out_shape=jax.ShapeDtypeStruct((slots, rows, slices), bf16),
        in_specs=[smem, vmem, vmem, vmem],
        out_specs=vmem,
        scratch_shapes=scratch,
        compiler_params=pltpu.CompilerParams(collective_id=0, has_side_effects=True),
    )(own_idx, packed, sinogram, weights)
    return pl.pallas_call(
        backward_kernel,
        out_shape=jax.ShapeDtypeStruct(volume.shape, f32),
        grid_spec=pltpu.PrefetchScalarGridSpec(
            num_scalar_prefetch=1,
            grid=(slots // block,),
            in_specs=[
                volume_spec,
                tile_spec,
                pl.BlockSpec((block, rows, slices), lambda s, *_: (s, 0, 0)),
            ],
            out_specs=pl.BlockSpec(volume.shape, lambda s, *_: (0, 0, 0)),
            scratch_shapes=[pltpu.VMEM((patch_tiles, slices + PIECE, cols), f32)],
        ),
    )(pixel, volume, projector, slot_residual)


def on_device(volume, projector, slot_ray, slot_pixel, sinogram, weight_index, weight_table):
    inners = lax.axis_size("inner")
    outers = lax.axis_size("outer")
    capacity = 2 * projector.shape[0] // inners
    dense = sinogram.shape[0] * outers <= capacity
    path = paired_path if outers == 2 and dense else general_path
    return path(volume, projector, slot_ray, slot_pixel, sinogram, weight_index, weight_table)


def solution(mesh):
    in_specs = (
        P(("group", "inner", "outer"), None, "cuts"),
        P(("inner", "outer"), None, None, None),
        P(("inner", "outer")),
        P(("inner", "outer"), None),
        P(("group", "inner", "outer"), None, "cuts"),
        P(("group", "inner", "outer"), None),
        P(),
    )
    out_specs = P(("group", "inner", "outer"), None, "cuts")
    return jax.shard_map(
        on_device, mesh=mesh, in_specs=in_specs, out_specs=out_specs, check_vma=False
    )
```

```python
import functools

import jax
import jax.numpy as jnp
from jax import lax
from jax.experimental import pallas as pl
from jax.experimental.pallas import tpu as pltpu
from jax.sharding import PartitionSpec as P

MESH = pl.DeviceIdType.MESH
PIECE = 16
LIMIT = 32000.0


def general_path(volume, projector, slot_ray, slot_pixel, sinogram, weight_index, weight_table):
    inners = lax.axis_size("inner")
    outers = lax.axis_size("outer")
    slot_count = projector.shape[0]
    per_slot = projector.shape[1]
    tile_rows = projector.shape[2]
    tile_cols = projector.shape[3]
    patch_tiles = volume.shape[0]
    slice_count = volume.shape[2]
    owned_rows = sinogram.shape[0]
    band_rows = owned_rows * outers
    capacity = 2 * slot_count // inners
    cell_count = inners * capacity
    target = slot_ray // band_rows
    offset = slot_ray % band_rows
    same_target = target[:, None] == target[None, :]
    earlier = jnp.arange(slot_count)[:, None] > jnp.arange(slot_count)[None, :]
    slot_rank = jnp.sum(jnp.logical_and(same_target, earlier), axis=1)
    position = target * capacity + slot_rank
    partial_value = jnp.zeros((slot_count, tile_rows, slice_count), jnp.float32)
    for column in range(per_slot):
        pixels = volume[slot_pixel[:, column]]
        partial_value = partial_value + jnp.einsum(
            "srp,spc->src", projector[:, column], pixels, preferred_element_type=jnp.float32
        )
    outgoing = (
        jnp.zeros((cell_count, tile_rows, slice_count), jnp.float32).at[position].set(partial_value)
    )
    labels = jnp.full((cell_count,), -1.0, jnp.float32).at[position].set(offset.astype(jnp.float32))
    arrived, arrived_rows = (
        lax.all_to_all(
            outgoing.reshape(inners, capacity, tile_rows, slice_count),
            "inner",
            split_axis=0,
            concat_axis=0,
            tiled=True,
        ),
        lax.all_to_all(
            labels.reshape(inners, capacity), "inner", split_axis=0, concat_axis=0, tiled=True
        ),
    )
    selector = (
        jnp.arange(band_rows, dtype=jnp.float32)[:, None] == arrived_rows.reshape(1, cell_count)
    ).astype(jnp.float32)
    block_sums = jnp.dot(
        selector,
        arrived.reshape(cell_count, tile_rows * slice_count),
        precision=lax.Precision.HIGHEST,
    ).reshape(band_rows, tile_rows, slice_count)
    classes = weight_table.shape[0]
    lookup = weight_index[:, :, None] == jnp.arange(classes)[None, None, :]
    weights = jnp.sum(
        jnp.where(lookup, weight_table[None, None, :], jnp.zeros((), weight_table.dtype)), axis=2
    )
    own_sums = lax.psum_scatter(block_sums, "outer", scatter_dimension=0, tiled=True)
    own_residual = (
        weights.astype(jnp.float32)[:, :, None] * (sinogram.astype(jnp.float32) - own_sums)
    ).astype(jnp.bfloat16)
    residual = lax.all_gather(own_residual, "outer", axis=0, tiled=True)
    picked = jnp.dot(
        selector.T.astype(jnp.bfloat16),
        residual.reshape(band_rows, tile_rows * slice_count),
        preferred_element_type=jnp.float32,
    ).astype(jnp.bfloat16)
    returned = lax.all_to_all(
        picked.reshape(inners, capacity, tile_rows, slice_count),
        "inner",
        split_axis=0,
        concat_axis=0,
        tiled=True,
    )
    slot_residual = returned.reshape(cell_count, tile_rows, slice_count)[position]
    owners = jnp.arange(patch_tiles)
    backward = jnp.zeros((patch_tiles, tile_cols, slice_count), jnp.float32)
    column_sum = jnp.zeros((patch_tiles, tile_cols), jnp.float32)
    for column in range(per_slot):
        member = (owners[:, None] == slot_pixel[None, :, column]).astype(jnp.float32)
        spread = jnp.einsum(
            "srp,src->spc", projector[:, column], slot_residual, preferred_element_type=jnp.float32
        )
        backward = backward + jnp.einsum(
            "ts,spc->tpc", member, spread, precision=lax.Precision.HIGHEST
        )
        column_sum = column_sum + jnp.dot(
            member,
            jnp.sum(projector[:, column], axis=1, dtype=jnp.float32),
            precision=lax.Precision.HIGHEST,
        )
    return volume.astype(jnp.float32) + backward / column_sum[:, :, None]


def exponent_of(largest):
    top = jnp.max(largest, axis=0, keepdims=True)
    exponent = jnp.ceil(jnp.log2(jnp.maximum(top, 1e-20) * (1.0 / LIMIT)))
    return jnp.broadcast_to(exponent, largest.shape)


def encode(value, inverse):
    return jnp.round(value * inverse).astype(jnp.int32).astype(jnp.int16)


def decode(coded):
    return coded.astype(jnp.int32).astype(jnp.float32)


def forward_kernel(
    ray_ref, pixel_ref, index_ref, table_ref, volume_ref, projector_ref, coded_ref, own_ref, wts_ref,
    packed_ref,
):
    step = pl.program_id(0)
    block, per_slot = projector_ref.shape[:2]
    slots, rows, slices = packed_ref.shape
    rays = own_ref.shape[0] - slots

    @pl.when(step == 0)
    def _():
        packed_ref[...] = jnp.zeros_like(packed_ref)

        def clear(r, carry):
            own_ref[slots + r] = slots
            return carry

        lax.fori_loop(0, rays, clear, 0, unroll=8)

        def enter(k, carry):
            s = slots - 1 - k
            own_ref[s] = ray_ref[s]
            own_ref[slots + ray_ref[s]] = s
            return carry

        lax.fori_loop(0, slots, enter, 0, unroll=4)
        index = index_ref[...]
        weight = jnp.zeros(index.shape, jnp.float32)
        table = table_ref[...].astype(jnp.float32)
        for k in range(table.shape[1]):
            weight = jnp.where(index == k, table[:, k : k + 1], weight)
        blank = jnp.zeros((rows - index.shape[0], rows), jnp.float32)
        wts_ref[...] = jnp.concatenate([weight, blank], axis=0).T

    for j in range(block):
        s = step * block + j
        pixels = jnp.concatenate(
            [volume_ref[pixel_ref[g, s]] for g in range(per_slot)], axis=0
        )
        tiles = jnp.concatenate([projector_ref[j, g] for g in range(per_slot)], axis=1)
        cell = own_ref[slots + ray_ref[s]]
        packed_ref[cell] += jnp.dot(tiles, pixels, preferred_element_type=jnp.float32)

    @pl.when(step == pl.num_programs(0) - 1)
    def _():
        largest = jnp.zeros((PIECE, slices), jnp.float32)
        for s in range(slots):
            for r in range(0, rows, PIECE):
                largest = jnp.maximum(largest, jnp.abs(packed_ref[s, r : r + PIECE]))
        exponent = exponent_of(largest)
        inverse = jnp.exp2(-exponent)
        for s in range(slots):
            for r in range(0, rows, PIECE):
                coded_ref[s, r : r + PIECE] = encode(packed_ref[s, r : r + PIECE], inverse)
        for r in range(0, rows, PIECE):
            coded_ref[slots, r : r + PIECE] = jnp.zeros((PIECE, slices), jnp.int16)
            coded_ref[slots + 1, r : r + PIECE] = exponent.astype(jnp.int32).astype(jnp.int16)


def backward_kernel(pixel_ref, volume_ref, projector_ref, residual_ref, out_ref, acc_ref):
    step = pl.program_id(0)
    block, per_slot, rows, cols = projector_ref.shape
    slices = residual_ref.shape[-1]

    @pl.when(step == 0)
    def _():
        acc_ref[...] = jnp.zeros_like(acc_ref)

    ones = jnp.ones((PIECE, rows), jnp.bfloat16)
    for j in range(block):
        s = step * block + j
        tall = jnp.concatenate([residual_ref[j].T, ones], axis=0)
        tiles = jnp.concatenate([projector_ref[j, g] for g in range(per_slot)], axis=1)
        spread = jnp.dot(tall, tiles, preferred_element_type=jnp.float32)
        for g in range(per_slot):
            acc_ref[pixel_ref[g, s]] += spread[:, g * cols : (g + 1) * cols]

    @pl.when(step == pl.num_programs(0) - 1)
    def _():
        for q in range(acc_ref.shape[0]):
            update = acc_ref[q, :slices] / acc_ref[q, slices : slices + 1]
            out_ref[q] = volume_ref[q].astype(jnp.float32) + update.T


def exchange_kernel(n, pieces, own_idx, packed, sino, wts, out_ref, *scratch):
    take = iter(scratch)
    mate_part = [next(take) for _ in range(pieces)]
    from_left, from_right, going, dense = (next(take) for _ in range(4))
    band_res = [next(take) for _ in range(pieces)]
    picked = [next(take) for _ in range(pieces)]
    landed = [next(take) for _ in range(pieces)]
    mate_sino, mate_wts, mate_idx = (next(take) for _ in range(3))
    x_send, x_recv, aux_send, aux_recv, sum_send, left_recv, right_recv = (
        next(take) for _ in range(7)
    )
    out_right, out_left, res_recv, pick_send, pick_recv = (next(take) for _ in range(5))

    slots, rows, slices = out_ref.shape
    owned = sino.shape[0]
    band = 2 * owned
    half = rows // 2
    depth = half // pieces
    i = lax.axis_index("inner")
    o = lax.axis_index("outer")
    mate = {"outer": 1 - o}
    right = {"inner": i + 1}
    left = {"inner": i - 1}

    def send(src, dst, ssem, rsem, device):
        return pltpu.make_async_remote_copy(
            src_ref=src, dst_ref=dst, send_sem=ssem, recv_sem=rsem, device_id=device,
            device_id_type=MESH,
        )

    barrier = pltpu.get_barrier_semaphore()
    pl.semaphore_signal(barrier, inc=1, device_id=mate, device_id_type=MESH)

    @pl.when(i > 0)
    def _():
        pl.semaphore_signal(barrier, inc=1, device_id=left, device_id_type=MESH)

    @pl.when(i < n - 1)
    def _():
        pl.semaphore_signal(barrier, inc=1, device_id=right, device_id_type=MESH)

    pl.semaphore_wait(barrier, jnp.where(i > 0, 2, 1) + jnp.where(i < n - 1, 1, 0))

    def mine(c):
        return pl.ds(pl.multiple_of(o * half + c * depth, depth), depth)

    def theirs(c):
        return pl.ds(pl.multiple_of((1 - o) * half + c * depth, depth), depth)

    def swap(c):
        return send(
            packed.at[:, theirs(c)],
            mate_part[c],
            x_send.at[c],
            x_recv.at[c],
            mate,
        )

    other_half = pl.ds(pl.multiple_of((1 - o) * half, half), half)
    aux = [
        send(sino.at[:, other_half], mate_sino, aux_send.at[0], aux_recv.at[0], mate),
        send(wts.at[other_half], mate_wts, aux_send.at[1], aux_recv.at[1], mate),
    ]
    table = send(own_idx, mate_idx, aux_send.at[2], aux_recv.at[2], mate)
    table.start()
    for c in range(pieces):
        swap(c).start()
        if c == pieces - 1:
            for copy in aux:
                copy.start()
    def local_scales(c):
        return (
            jnp.exp2(decode(packed[slots + 1, mine(c), :])),
            jnp.exp2(decode(mate_part[c][slots + 1])),
        )

    def local(c, r, scales):
        return (
            decode(packed[own_idx[slots + r], mine(c), :]) * scales[0]
            + decode(mate_part[c][mate_idx[slots + r]]) * scales[1]
        )

    def loop(count, body):
        def step(t, carry):
            body(t)
            return carry

        lax.fori_loop(0, count, step, 0, unroll=4)

    def go_right(c, b):
        return send(
            going.at[c, b], from_left.at[c, b], sum_send.at[c, b], left_recv.at[c, b], right
        )

    def go_left(c, b):
        return send(
            going.at[c, b], from_right.at[c, b], sum_send.at[c, b], right_recv.at[c, b], left
        )

    def gather(c):
        swap(c).wait_recv()
        scales = local_scales(c)

        def fill(r):
            dense[c, r] = local(c, r, scales)

        loop(n * band, fill)

    def hop(c, b, to_right):
        copy = (go_right if to_right else go_left)(c, b)
        arrived = from_left if to_right else from_right

        def widest(t, largest):
            return jnp.maximum(largest, jnp.abs(dense[c, b * band + t]))

        @pl.when(i > 0 if to_right else i < n - 1)
        def _():
            copy.wait_recv()
            scale = jnp.exp2(decode(arrived[c, b, band]))

            def add(t):
                dense[c, b * band + t] += decode(arrived[c, b, t]) * scale

            loop(band, add)

        exponent = exponent_of(
            lax.fori_loop(0, band, widest, jnp.zeros((depth, slices), jnp.float32), unroll=4)
        )
        inverse = jnp.exp2(-exponent)

        def pack(t):
            going[c, b, t] = encode(dense[c, b * band + t], inverse)

        loop(band, pack)
        going[c, b, band] = exponent.astype(jnp.int32).astype(jnp.int16)
        copy.start()

    def sums(step):
        def rightward(far, carry):
            c = step - i - far
            pl.when(jnp.logical_and(c >= 0, c < pieces))(lambda: hop(c, n - 1 - far, True))
            return carry

        def leftward(far, carry):
            c = step - (n - 1 - i) - far
            pl.when(jnp.logical_and(c >= 0, c < pieces))(lambda: hop(c, far, False))
            return carry

        lax.fori_loop(0, n - 1 - i, rightward, 0)
        lax.fori_loop(0, i, leftward, 0)

    def share_right(c, b):
        part = band_res[c].at[pl.ds(pl.multiple_of(b * band, band), band)]
        return send(part, part, out_right.at[c, b], res_recv.at[c, b], right)

    def share_left(c, b):
        part = band_res[c].at[pl.ds(pl.multiple_of(b * band, band), band)]
        return send(part, part, out_left.at[c, b], res_recv.at[c, b], left)

    def finish(c):
        @pl.when(i > 0)
        def _():
            go_right(c, i).wait_recv()

            scale = jnp.exp2(decode(from_left[c, i, band]))

            def add(t):
                dense[c, i * band + t] += decode(from_left[c, i, t]) * scale

            loop(band, add)

        @pl.when(i < n - 1)
        def _():
            go_left(c, i).wait_recv()

            scale = jnp.exp2(decode(from_right[c, i, band]))

            def add(t):
                dense[c, i * band + t] += decode(from_right[c, i, t]) * scale

            loop(band, add)

        if c == 0:
            for copy in aux:
                copy.wait_recv()
        for j in range(owned):
            t = o * owned + j
            weight = wts[mine(c), j : j + 1]
            value = weight * (sino[j, mine(c), :].astype(jnp.float32) - dense[c, i * band + t])
            band_res[c][i * band + t] = value.astype(jnp.bfloat16)
            t = (1 - o) * owned + j
            rows_here = pl.ds(c * depth, depth)
            weight = mate_wts[rows_here, j : j + 1]
            value = weight * (mate_sino[j, rows_here, :].astype(jnp.float32) - dense[c, i * band + t])
            band_res[c][i * band + t] = value.astype(jnp.bfloat16)

        @pl.when(i < n - 1)
        def _():
            share_right(c, i).start()

        @pl.when(i > 0)
        def _():
            share_left(c, i).start()

    def relay(c, d):
        @pl.when(i - d >= 0)
        def _():
            share_right(c, i - d).wait_recv()

            @pl.when(i < n - 1)
            def _():
                share_right(c, i - d).start()

        @pl.when(i + d <= n - 1)
        def _():
            share_left(c, i + d).wait_recv()

            @pl.when(i > 0)
            def _():
                share_left(c, i + d).start()

    def give(c):
        return send(picked[c], landed[c], pick_send.at[c], pick_recv.at[c], mate)

    def pick(c):
        def for_mate(k):
            picked[c][k] = band_res[c][mate_idx[k]]

        loop(slots, for_mate)
        give(c).start()

        def for_self(k):
            out_ref[k, mine(c), :] = band_res[c][own_idx[k]]

        loop(slots, for_self)

    def collect(c):
        give(c).wait_recv()

        def copy_in(k):
            out_ref[k, theirs(c), :] = landed[c][k]

        loop(slots, copy_in)

    table.wait_recv()
    for step in range(pieces + 2 * (n - 1)):
        if step < pieces:
            gather(step)
        if step < pieces + n - 1:
            sums(step)
        for d in range(n):
            c = step - (n - 1) - d
            if 0 <= c < pieces:
                if d == 0:
                    finish(c)
                else:
                    relay(c, d)
                if d == n - 1:
                    pick(c)
    for c in range(pieces):
        collect(c)

    for copy in aux + [table]:
        copy.wait_send()
    for c in range(pieces):
        swap(c).wait_send()
        give(c).wait_send()
        for b in range(n):

            @pl.when(b > i)
            def _():
                go_right(c, b).wait_send()

            @pl.when(b < i)
            def _():
                go_left(c, b).wait_send()

            @pl.when(jnp.logical_and(b <= i, i < n - 1))
            def _():
                share_right(c, b).wait_send()

            @pl.when(jnp.logical_and(b >= i, i > 0))
            def _():
                share_left(c, b).wait_send()


def paired_path(volume, projector, slot_ray, slot_pixel, sinogram, weight_index, weight_table):
    n = lax.axis_size("inner")
    slots, per_slot, rows, cols = projector.shape
    patch_tiles, _, slices = volume.shape
    owned = sinogram.shape[0]
    band = 2 * owned
    rays = n * band
    pieces = rows // 2 // PIECE
    depth = PIECE
    pixel = slot_pixel.T
    classes = weight_table.shape[0]
    block = 8
    tile_spec = pl.BlockSpec((block, per_slot, rows, cols), lambda s, *_: (s, 0, 0, 0))
    volume_spec = pl.BlockSpec(volume.shape, lambda s, *_: (0, 0, 0))
    whole = lambda shape: pl.BlockSpec(shape, lambda s, *_: (0,) * len(shape))
    coded_shape = (slots + 2, rows, slices)
    packed, own_idx, weights = pl.pallas_call(
        forward_kernel,
        out_shape=(
            jax.ShapeDtypeStruct(coded_shape, jnp.int16),
            jax.ShapeDtypeStruct((slots + rays,), jnp.int32),
            jax.ShapeDtypeStruct((rows, rows), jnp.float32),
        ),
        grid_spec=pltpu.PrefetchScalarGridSpec(
            num_scalar_prefetch=2,
            grid=(slots // block,),
            in_specs=[whole(weight_index.shape), whole((1, classes)), volume_spec, tile_spec],
            out_specs=(
                whole(coded_shape),
                pl.BlockSpec(memory_space=pltpu.SMEM),
                whole((rows, rows)),
            ),
            scratch_shapes=[pltpu.VMEM((slots, rows, slices), jnp.float32)],
        ),
    )(slot_ray, pixel, weight_index, weight_table.reshape(1, classes), volume, projector)
    f32, bf16 = jnp.float32, jnp.bfloat16
    dma = pltpu.SemaphoreType.DMA
    vmem = pl.BlockSpec(memory_space=pltpu.VMEM)
    smem = pl.BlockSpec(memory_space=pltpu.SMEM)
    scratch = (
        [pltpu.VMEM((slots + 2, depth, slices), jnp.int16)] * pieces
        + [pltpu.VMEM((pieces, n, band + 1, depth, slices), jnp.int16)] * 3
        + [pltpu.VMEM((pieces, rays, depth, slices), f32)]
        + [pltpu.VMEM((rays, depth, slices), bf16)] * pieces
        + [pltpu.VMEM((slots, depth, slices), bf16)] * (2 * pieces)
        + [pltpu.VMEM((owned, rows // 2, slices), bf16), pltpu.VMEM((rows // 2, 128), f32)]
        + [pltpu.SMEM((slots + rays,), jnp.int32)]
        + [dma((pieces,)), dma((pieces,)), dma((3,)), dma((3,))]
        + [dma((pieces, n))] * 6
        + [dma((pieces,)), dma((pieces,))]
    )
    slot_residual = pl.pallas_call(
        functools.partial(exchange_kernel, n, pieces),
        out_shape=jax.ShapeDtypeStruct((slots, rows, slices), bf16),
        in_specs=[smem, vmem, vmem, vmem],
        out_specs=vmem,
        scratch_shapes=scratch,
        compiler_params=pltpu.CompilerParams(collective_id=0, has_side_effects=True),
    )(own_idx, packed, sinogram, weights)
    return pl.pallas_call(
        backward_kernel,
        out_shape=jax.ShapeDtypeStruct(volume.shape, f32),
        grid_spec=pltpu.PrefetchScalarGridSpec(
            num_scalar_prefetch=1,
            grid=(slots // block,),
            in_specs=[
                volume_spec,
                tile_spec,
                pl.BlockSpec((block, rows, slices), lambda s, *_: (s, 0, 0)),
            ],
            out_specs=pl.BlockSpec(volume.shape, lambda s, *_: (0, 0, 0)),
            scratch_shapes=[pltpu.VMEM((patch_tiles, slices + PIECE, cols), f32)],
        ),
    )(pixel, volume, projector, slot_residual)


def on_device(volume, projector, slot_ray, slot_pixel, sinogram, weight_index, weight_table):
    inners = lax.axis_size("inner")
    outers = lax.axis_size("outer")
    capacity = 2 * projector.shape[0] // inners
    dense = sinogram.shape[0] * outers <= capacity
    path = paired_path if outers == 2 and dense else general_path
    return path(volume, projector, slot_ray, slot_pixel, sinogram, weight_index, weight_table)


def solution(mesh):
    in_specs = (
        P(("group", "inner", "outer"), None, "cuts"),
        P(("inner", "outer"), None, None, None),
        P(("inner", "outer")),
        P(("inner", "outer"), None),
        P(("group", "inner", "outer"), None, "cuts"),
        P(("group", "inner", "outer"), None),
        P(),
    )
    out_specs = P(("group", "inner", "outer"), None, "cuts")
    return jax.shard_map(
        on_device, mesh=mesh, in_specs=in_specs, out_specs=out_specs, check_vma=False
    )
```
